32 devices in a mesh: dp: 8 (over z, y), mod: 4 (over x, core).
Axes of the slice: x: 2, y: 2, z: 4, core: 2. Of those that a mesh axis runs over, the one named last changes fastest.
Arguments:
- text_emb: bfloat16 [64, 384, 768], P(('dp', 'mod')), may hold values from -6 to 6
- feature_maps: bfloat16 [64, 320, 256], P(('dp', 'mod')), may hold values from -6 to 6
- boxes: int32 [64, 128, 4], P(('dp', 'mod')), may hold values from 0 to 16, as said below
- row_counts: int32 [64, 2], P('dp'), may hold values from 1 to 384, as said below
- w_roi: bfloat16 [512, 768], P('dp'), may hold values from -0.25 to 0.25
- bn_gain: bfloat16 [768], P('dp'), may hold values from 0.5 to 1.5
- bn_bias: bfloat16 [768], P('dp'), may hold values from -1.75 to 1.75
- w_query: bfloat16 [768, 768], P('dp'), may hold values from -0.21875 to 0.21875
- w_key: bfloat16 [768, 768], P('dp'), may hold values from -0.21875 to 0.21875
- w_value: bfloat16 [768, 768], P('dp'), may hold values from -0.21875 to 0.21875
- b_query: bfloat16 [768], P('dp'), may hold values from -3 to 3
- b_value: bfloat16 [768], P('dp'), may hold values from -3 to 3
- w_out: bfloat16 [768, 768], P('dp'), may hold values from -0.625 to 0.625
- b_out: bfloat16 [768], P('dp'), may hold values from -3 to 3
- ln1_gain: bfloat16 [768], P('dp'), may hold values from 0.5 to 1.5
- ln1_bias: bfloat16 [768], P('dp'), may hold values from -1.75 to 1.75
- w_up: bfloat16 [768, 3072], P('dp'), may hold values from -0.21875 to 0.21875
- b_up: bfloat16 [3072], P('dp'), may hold values from -3 to 3
- w_down: bfloat16 [3072, 768], P('dp'), may hold values from -0.109375 to 0.109375
- b_down: bfloat16 [768], P('dp'), may hold values from -1.75 to 1.75
- ln2_gain: bfloat16 [768], P('dp'), may hold values from 0.5 to 1.5
- ln2_bias: bfloat16 [768], P('dp'), may hold values from -1.75 to 1.75
- out_grad_text: bfloat16 [64, 384, 768], P(('dp', 'mod')), may hold values from -6 to 6
- out_grad_roi: bfloat16 [64, 128, 768], P(('dp', 'mod')), may hold values from -6 to 6
Outputs:
- out_text: bfloat16 [64, 384, 768], P(('dp', 'mod'))
- out_roi: bfloat16 [64, 128, 768], P(('dp', 'mod'))
- grad_text: float32 [64, 384, 768], P(('dp', 'mod'))
- grad_maps: float32 [64, 320, 256], P(('dp', 'mod'))
- grad_w_roi: float32 [512, 768], P('dp')
- grad_bn_gain: float32 [768], P('dp')
- grad_bn_bias: float32 [768], P('dp')
- grad_w_query: float32 [768, 768], P('dp')
- grad_w_key: float32 [768, 768], P('dp')
- grad_w_value: float32 [768, 768], P('dp')
- grad_b_query: float32 [768], P('dp')
- grad_b_value: float32 [768], P('dp')
- grad_w_out: float32 [768, 768], P('dp')
- grad_b_out: float32 [768], P('dp')
- grad_ln1_gain: float32 [768], P('dp')
- grad_ln1_bias: float32 [768], P('dp')
- grad_w_up: float32 [768, 3072], P('dp')
- grad_b_up: float32 [3072], P('dp')
- grad_w_down: float32 [3072, 768], P('dp')
- grad_b_down: float32 [768], P('dp')
- grad_ln2_gain: float32 [768], P('dp')
- grad_ln2_bias: float32 [768], P('dp')
The draws below stay inside these ranges and needn't reach their ends.
Inputs may be any that keep to these rules, and one draw needn't show every extreme that they name: `boxes`: each box is x0, y0, x1, y1 on the 16 x 16 fine grid with x0 < x1 and y0 < y1; a box covering the whole grid occurs. `row_counts`: column 0 counts a page's live text rows, at most 384; column 1 its live 128 rows, at most 128; both bounds are reached; live rows are the first slots.
All inputs are finite; a program needn't handle non-finite values.
Results may differ from the reference program's by a relative error of at most 0.022.
Values may be sent and summed in bfloat16 or wider, within the bound.
A program may use at most 256 MiB of HBM per device.

```python
import jax
import jax.numpy as jnp
from jax import lax

D = 768
HEADS = 12
HD = 64
FF = 3072
CH = 256
FINE = 16
COARSE = 8
CELLS = 320
TXT = 384
ROI = 128
HALF_GRP = 4
PAGES = 64


def draw_boxes(key, part):
    key_left, key_top, key_wide, key_tall = jax.random.split(key, 4)
    left_edge = jax.random.randint(key_left, (PAGES, ROI), 0, FINE)
    top_edge = jax.random.randint(key_top, (PAGES, ROI), 0, FINE)
    right_edge = left_edge + jax.random.randint(key_wide, (PAGES, ROI), 1, FINE + 1 - left_edge)
    bottom_edge = top_edge + jax.random.randint(key_tall, (PAGES, ROI), 1, FINE + 1 - top_edge)
    stacked = jnp.stack([left_edge, top_edge, right_edge, bottom_edge], -1).astype(jnp.int32)
    whole_box = jnp.array([0, 0, FINE, FINE], dtype=jnp.int32)
    return stacked.at[0, 0].set(whole_box)


def draw_row_counts(key, part):
    key_text, key_region = jax.random.split(key)
    text_rows = jax.random.randint(key_text, (PAGES,), 1, TXT + 1)
    region_rows = jax.random.randint(key_region, (PAGES,), 1, ROI + 1)
    text_rows = text_rows.at[0].set(TXT)
    region_rows = region_rows.at[0].set(ROI)
    return jnp.stack([text_rows, region_rows], -1).astype(jnp.int32)


def block_scale(key, extent, shards, least, high):
    gain = 1.0
    for position, blocks in shards:
        heights = jax.random.uniform(jax.random.fold_in(jax.random.fold_in(key, 6), position), (blocks,), jnp.float32, least / len(shards), high / len(shards))
        gain = gain * jnp.repeat(jnp.exp(heights), extent[position] // blocks).reshape((-1,) + (1,) * (len(extent) - 1 - position))
    return gain


def noise(stream_key, shape, deviation, most, cuts=(), held_as=jnp.bfloat16):
    gain = block_scale(stream_key, shape, cuts, -0.22, 0.18) if cuts else 1.0
    values = jax.random.normal(stream_key, shape, jnp.float32) * deviation * gain
    return jnp.minimum(jnp.maximum(values, -most), most).astype(held_as)


def setup_inputs(seed: int = 0) -> dict:
    seeds = jax.random.split(jax.random.key(seed), 25)
    return {
        "text_emb": noise(seeds[0], (PAGES, TXT, D), 1.0, 6.0, ((0, 32),)),
        "feature_maps": noise(seeds[1], (PAGES, CELLS, CH), 1.0, 6.0, ((0, 32),)),
        "boxes": draw_boxes(jax.random.fold_in(seeds[24], 71), 0),
        "row_counts": draw_row_counts(jax.random.fold_in(seeds[24], 71), 0),
        "w_roi": noise(seeds[4], (2 * CH, D), (2 * CH) ** -0.5, 0.25, ((0, 8),)),
        "bn_gain": jnp.clip(1.0 + 0.1 * jax.random.normal(seeds[5], (D,), jnp.float32), 0.5, 1.5).astype(jnp.bfloat16),
        "bn_bias": noise(seeds[6], (D,), 0.3, 1.75, ((0, 8),)),
        "w_query": noise(seeds[7], (D, D), D ** -0.5, 0.21875, ((0, 8),)),
        "w_key": noise(seeds[8], (D, D), D ** -0.5, 0.21875, ((0, 8),)),
        "w_value": noise(seeds[9], (D, D), D ** -0.5, 0.21875, ((0, 8),)),
        "b_query": noise(seeds[10], (D,), 0.5, 3.0, ((0, 8),)),
        "b_value": noise(seeds[11], (D,), 0.5, 3.0, ((0, 8),)),
        "w_out": noise(seeds[12], (D, D), (D // 8) ** -0.5, 0.625, ((0, 8),)),
        "b_out": noise(seeds[13], (D,), 0.5, 3.0, ((0, 8),)),
        "ln1_gain": jnp.clip(1.0 + 0.1 * jax.random.normal(seeds[14], (D,), jnp.float32), 0.5, 1.5).astype(jnp.bfloat16),
        "ln1_bias": noise(seeds[15], (D,), 0.3, 1.75, ((0, 8),)),
        "w_up": noise(seeds[16], (D, FF), D ** -0.5, 0.21875, ((0, 8),)),
        "b_up": noise(seeds[17], (FF,), 0.5, 3.0, ((0, 8),)),
        "w_down": noise(seeds[18], (FF, D), FF ** -0.5, 0.109375, ((0, 8),)),
        "b_down": noise(seeds[19], (D,), 0.3, 1.75, ((0, 8),)),
        "ln2_gain": jnp.clip(1.0 + 0.1 * jax.random.normal(seeds[20], (D,), jnp.float32), 0.5, 1.5).astype(jnp.bfloat16),
        "ln2_bias": noise(seeds[21], (D,), 0.3, 1.75, ((0, 8),)),
        "out_grad_text": noise(seeds[22], (PAGES, TXT, D), 1.0, 6.0, ((0, 32),)),
        "out_grad_roi": noise(seeds[23], (PAGES, ROI, D), 1.0, 6.0, ((0, 32),)),
    }


@jax.custom_vjp
def low(v):
    return lax.optimization_barrier(v.astype(jnp.bfloat16)).astype(jnp.float32)

@jax.custom_vjp
def low_back(v):
    return v

def low_keep(v):
    return (low(v), None)

def low_pass(kept, grad):
    return (grad,)

def back_keep(v):
    return (v, None)

def back_low(kept, grad):
    return (low(grad),)
low.defvjp(low_keep, low_pass)
low_back.defvjp(back_keep, back_low)

def highest(form, left_mat, right_mat):
    return jnp.einsum(form, left_mat, right_mat, precision=lax.Precision.HIGHEST, preferred_element_type=jnp.float32)

def layer_norm(hidden_in, gain_vec, bias_vec):
    average = lax.optimization_barrier(jnp.mean(hidden_in, axis=-1, keepdims=True))
    centered = hidden_in - average
    variance = lax.optimization_barrier(jnp.mean(centered * centered, axis=-1, keepdims=True))
    return centered * lax.rsqrt(variance + 1e-05) * gain_vec + bias_vec

def exact_gelu(hidden_in):
    return jax.nn.gelu(hidden_in, approximate=False)

def slot_order():
    page_index = jnp.arange(PAGES, dtype=jnp.int32)
    return jnp.where(page_index // HALF_GRP % 2 == 0, page_index + HALF_GRP, page_index - HALF_GRP).astype(jnp.int32)

def box_masks(boxes):
    left_edge = boxes[..., 0:1]
    top_edge = boxes[..., 1:2]
    right_edge = boxes[..., 2:3]
    bottom_edge = boxes[..., 3:4]
    fine_cell = jnp.arange(FINE * FINE, dtype=jnp.int32)
    fine_row = fine_cell // FINE
    fine_col = fine_cell % FINE
    inside_fine = (fine_col >= left_edge) & (fine_col < right_edge) & (fine_row >= top_edge) & (fine_row < bottom_edge)
    coarse_cell = jnp.arange(COARSE * COARSE, dtype=jnp.int32)
    coarse_row = coarse_cell // COARSE
    coarse_col = coarse_cell % COARSE
    inside_coarse = (coarse_col >= left_edge // 2) & (coarse_col < (right_edge + 1) // 2) & (coarse_row >= top_edge // 2) & (coarse_row < (bottom_edge + 1) // 2)
    return (inside_coarse, inside_fine)

def page_layer(rows_in, live_in, params):
    query_weight, key_weight, value_weight, query_bias, value_bias, out_weight, out_bias, first_gain, first_bias, up_weight, up_bias, down_weight, down_bias, second_gain, second_bias = params
    block_size, slot_count, model_width = rows_in.shape
    queries = low(low_back(highest('bsd,de->bse', rows_in, query_weight) + query_bias)).reshape(block_size, slot_count, HEADS, HD)
    key_rows = low(low_back(highest('bsd,de->bse', rows_in, key_weight))).reshape(block_size, slot_count, HEADS, HD)
    values = low(low_back(highest('bsd,de->bse', rows_in, value_weight) + value_bias)).reshape(block_size, slot_count, HEADS, HD)
    raw_scores = low_back(highest('bqhe,bkhe->bhqk', queries, key_rows) * HD ** (-0.5))
    scores = jnp.where(live_in[:, None, None, :], raw_scores, -1e+30)
    weights_soft = low(jax.nn.softmax(scores, axis=-1))
    context = low(low_back(highest('bhqk,bkhe->bqhe', weights_soft, values).reshape(block_size, slot_count, model_width)))
    attended = low_back(highest('bsd,de->bse', context, out_weight) + out_bias)
    normed = layer_norm(rows_in + attended, first_gain, first_bias)
    hidden = low_back(highest('bsd,df->bsf', low(normed), up_weight) + up_bias)
    activated = low(exact_gelu(hidden))
    mixed = low_back(highest('bsf,fd->bsd', activated, down_weight) + down_bias)
    return layer_norm(normed + mixed, second_gain, second_bias) * live_in.astype(jnp.float32)[:, :, None]

def reference(text_emb, feature_maps, boxes, row_counts, w_roi, bn_gain, bn_bias, w_query, w_key, w_value, b_query, b_value, w_out, b_out, ln1_gain, ln1_bias, w_up, b_up, w_down, b_down, ln2_gain, ln2_bias, out_grad_text, out_grad_roi):
    order = slot_order()
    inside_coarse, inside_fine = box_masks(boxes[order])
    coarse_mask = inside_coarse.astype(jnp.float32)
    fine_mask = inside_fine.astype(jnp.float32)
    text_live = jnp.arange(TXT, dtype=jnp.int32)[None, :] < row_counts[:, 0:1]
    roi_live = jnp.arange(ROI, dtype=jnp.int32)[None, :] < row_counts[:, 1:2]
    live = jnp.concatenate([text_live, roi_live], 1)
    roi_mask = roi_live.astype(jnp.float32)[:, :, None]
    coarse_cells = COARSE * COARSE

    def forward(text_in, maps_in, *params):
        roi_proj = params[0]
        norm_gain = params[1]
        norm_bias = params[2]
        page_maps = maps_in[order]
        coarse_pool = highest('prc,pcf->prf', coarse_mask, page_maps[:, :coarse_cells]) / lax.optimization_barrier(jnp.sum(coarse_mask, -1, keepdims=True))
        fine_pool = highest('prc,pcf->prf', fine_mask, page_maps[:, coarse_cells:]) / lax.optimization_barrier(jnp.sum(fine_mask, -1, keepdims=True))
        pooled = low(low_back(jnp.concatenate([coarse_pool, fine_pool], -1)))
        projected = low_back(highest('prc,cd->prd', pooled, roi_proj))
        number = jnp.sum(roi_mask)
        average = lax.optimization_barrier(jnp.sum(projected * roi_mask, axis=(0, 1))) / number
        variance = lax.optimization_barrier(jnp.sum(projected * projected * roi_mask, axis=(0, 1))) / number - average * average
        standard = (projected - average) * lax.rsqrt(variance + 1e-05)
        roi_rows = low(standard * norm_gain + norm_bias)
        page_rows = jnp.concatenate([text_in, roi_rows], 1)
        block_rows = page_rows.reshape(PAGES // 8, 8, TXT + ROI, D)
        block_live = live.reshape(PAGES // 8, 8, TXT + ROI)
        layer_params = params[3:]

        def one_block(block_pair):
            return page_layer(block_pair[0], block_pair[1], layer_params)
        outputs = lax.map(jax.checkpoint(one_block), (block_rows, block_live)).reshape(PAGES, TXT + ROI, D)
        return (outputs[:, :TXT], outputs[:, TXT:][order])
    floats = tuple((argument.astype(jnp.float32) for argument in (text_emb, feature_maps, w_roi, bn_gain, bn_bias, w_query, w_key, w_value, b_query, b_value, w_out, b_out, ln1_gain, ln1_bias, w_up, b_up, w_down, b_down, ln2_gain, ln2_bias)))
    outputs, backward = jax.vjp(forward, *floats)
    grads = backward((out_grad_text.astype(jnp.float32), out_grad_roi.astype(jnp.float32)))
    return (outputs[0].astype(jnp.bfloat16), outputs[1].astype(jnp.bfloat16), grads[0], grads[1], grads[2], grads[3], grads[4], grads[5], grads[6], grads[7], grads[8], grads[9], grads[10], grads[11], grads[12], grads[13], grads[14], grads[15], grads[16], grads[17], grads[18], grads[19])
```

```python
import functools

import jax
import jax.numpy as jnp
from jax import lax
from jax.experimental import pallas as pl
from jax.experimental.pallas import tpu as pltpu
from jax.sharding import PartitionSpec as P

HEADS = 12
FINE = 16
COARSE = 8
PAIR = 128
BOTH = ("dp", "mod")


def swapped(block, axis, distance):
    count = lax.axis_size(axis)
    route = []
    for low in range(count):
        high = low | 1 << distance
        if high != low and high < count:
            route += [(low, high), (high, low)]
    return lax.ppermute(block, axis, route)


def product(left_mat, right_mat):
    return jnp.dot(left_mat, right_mat, preferred_element_type=jnp.float32)


def inner_rows(left_mat, right_mat):
    return lax.dot_general(
        left_mat, right_mat, (((0,), (0,)), ((), ())), preferred_element_type=jnp.float32
    )


def outer_cols(left_mat, right_mat):
    return lax.dot_general(
        left_mat, right_mat, (((1,), (1,)), ((), ())), preferred_element_type=jnp.float32
    )


def norm_forward(hidden_in, gain_vec, bias_vec):
    average = jnp.mean(hidden_in, axis=-1, keepdims=True)
    centered = hidden_in - average
    variance = jnp.mean(centered * centered, axis=-1, keepdims=True)
    inverse = lax.rsqrt(variance + 1e-05)
    return centered * inverse * gain_vec + bias_vec, average, inverse


def norm_backward(grad_out, hidden_in, average, inverse, gain_vec):
    standard = (hidden_in - average) * inverse
    grad_gain = jnp.sum(grad_out * standard, 0)
    grad_bias = jnp.sum(grad_out, 0)
    scaled = grad_out * gain_vec
    mean_scaled = jnp.mean(scaled, axis=-1, keepdims=True)
    mean_cross = jnp.mean(scaled * standard, axis=-1, keepdims=True)
    grad_hidden = inverse * (scaled - mean_scaled - standard * mean_cross)
    return grad_hidden, grad_gain, grad_bias


def box_masks(boxes):
    left_edge = boxes[..., 0:1]
    top_edge = boxes[..., 1:2]
    right_edge = boxes[..., 2:3]
    bottom_edge = boxes[..., 3:4]
    fine_cell = jnp.arange(FINE * FINE, dtype=jnp.int32)
    fine_row = fine_cell // FINE
    fine_col = fine_cell % FINE
    inside_fine = (
        (fine_col >= left_edge)
        & (fine_col < right_edge)
        & (fine_row >= top_edge)
        & (fine_row < bottom_edge)
    )
    coarse_cell = jnp.arange(COARSE * COARSE, dtype=jnp.int32)
    coarse_row = coarse_cell // COARSE
    coarse_col = coarse_cell % COARSE
    inside_coarse = (
        (coarse_col >= left_edge // 2)
        & (coarse_col < (right_edge + 1) // 2)
        & (coarse_row >= top_edge // 2)
        & (coarse_row < (bottom_edge + 1) // 2)
    )
    coarse_area = jnp.sum(inside_coarse.astype(jnp.float32), -1, keepdims=True)
    fine_area = jnp.sum(inside_fine.astype(jnp.float32), -1, keepdims=True)
    return inside_coarse, inside_fine, coarse_area, fine_area


def key_live(counts_ref, page, text_slots, slots):
    col = lax.broadcasted_iota(jnp.int32, (1, slots), 1)
    text_count = counts_ref[page, 0]
    roi_count = counts_ref[page, 1]
    return (col < text_count) | ((col >= text_slots) & (col < text_slots + roi_count))


def attend_kernel(text_slots, scale, counts_ref, query_ref, key_ref, value_ref, out_ref, log_ref):
    slots = query_ref.shape[0]
    live = key_live(counts_ref, pl.program_id(0), text_slots, slots)
    lane = lax.broadcasted_iota(jnp.int32, (1, PAIR), 1)
    query = query_ref[...] * scale
    keys = key_ref[...]
    values = value_ref[...]
    parts = []
    logs = []
    for head in range(2):
        mine = (lane // (PAIR // 2)) == head
        masked = jnp.where(mine, query, jnp.zeros_like(query))
        scores = jnp.where(live, outer_cols(masked, keys), -1e30)
        highest = jnp.max(scores, -1, keepdims=True)
        exponent = jnp.exp(scores - highest)
        total = jnp.sum(exponent, -1, keepdims=True)
        weights = (exponent * (1.0 / total)).astype(jnp.bfloat16)
        parts.append(product(weights, values))
        logs.append(highest + jnp.log(total))
    first = lane < PAIR // 2
    out_ref[...] = jnp.where(first, parts[0], parts[1]).astype(jnp.bfloat16)
    log_ref[...] = jnp.where(first, logs[0], logs[1])


def attend_back_kernel(
    text_slots,
    scale,
    counts_ref,
    query_ref,
    key_ref,
    value_ref,
    grad_ref,
    log_ref,
    grad_query_ref,
    grad_key_ref,
    grad_value_ref,
):
    slots = query_ref.shape[0]
    live = key_live(counts_ref, pl.program_id(0), text_slots, slots)
    lane = lax.broadcasted_iota(jnp.int32, (1, PAIR), 1)
    query = query_ref[...] * scale
    keys = key_ref[...]
    values = value_ref[...]
    grad = grad_ref[...]
    logs = log_ref[...]
    queries_out = []
    keys_out = []
    values_out = []
    for head in range(2):
        mine = (lane // (PAIR // 2)) == head
        masked = jnp.where(mine, query, jnp.zeros_like(query))
        grad_mine = jnp.where(mine, grad, jnp.zeros_like(grad))
        log_col = logs[:, head * (PAIR // 2) : head * (PAIR // 2) + 1]
        weights = jnp.exp(jnp.where(live, outer_cols(masked, keys), -1e30) - log_col)
        grad_weights = outer_cols(grad_mine, values)
        delta = jnp.sum(grad_weights * weights, -1, keepdims=True)
        grad_scores = (weights * (grad_weights - delta)).astype(jnp.bfloat16)
        values_out.append(inner_rows(weights.astype(jnp.bfloat16), grad))
        queries_out.append(product(grad_scores, keys))
        keys_out.append(inner_rows(grad_scores, query))
    first = lane < PAIR // 2
    grad_query_ref[...] = (jnp.where(first, queries_out[0], queries_out[1]) * scale).astype(
        jnp.bfloat16
    )
    grad_key_ref[...] = jnp.where(first, keys_out[0], keys_out[1]).astype(jnp.bfloat16)
    grad_value_ref[...] = jnp.where(first, values_out[0], values_out[1]).astype(jnp.bfloat16)


def attention_call(kernel, counts, operands, out_types, page_count, flops):
    rows, width = operands[0].shape
    slots = rows // page_count
    spec = pl.BlockSpec((slots, PAIR), lambda page, pair, counts_ref: (page, pair))
    return pl.pallas_call(
        kernel,
        out_shape=tuple(jax.ShapeDtypeStruct((rows, width), kind) for kind in out_types),
        grid_spec=pltpu.PrefetchScalarGridSpec(
            num_scalar_prefetch=1,
            grid=(page_count, width // PAIR),
            in_specs=[spec] * len(operands),
            out_specs=tuple([spec] * len(out_types)),
        ),
        cost_estimate=pl.CostEstimate(
            flops=flops,
            bytes_accessed=rows * width * 2 * (len(operands) + len(out_types)),
            transcendentals=rows * slots * HEADS,
        ),
        compiler_params=pltpu.CompilerParams(
            dimension_semantics=("arbitrary", "arbitrary"), vmem_limit_bytes=40 << 20
        ),
    )(counts, *operands)


def gather_all(shard):
    mod_size = lax.axis_size("mod")
    piece = shard.shape[0] // mod_size
    mine = lax.dynamic_slice_in_dim(shard, lax.axis_index("mod") * piece, piece, 0)
    full = lax.all_gather(mine, BOTH, axis=0, tiled=True)
    return full.reshape(-1, *shard.shape)


def scatter_sum(stacked):
    dp_size, rows, width = stacked.shape
    part = lax.psum_scatter(
        stacked.reshape(dp_size * rows, width), BOTH, scatter_dimension=0, tiled=True
    )
    return lax.all_gather(part, "mod", axis=0, tiled=True)


def total_sum(stats):
    return lax.psum(stats, BOTH)


def body(
    text_emb,
    feature_maps,
    boxes,
    row_counts,
    w_roi,
    bn_gain,
    bn_bias,
    w_query,
    w_key,
    w_value,
    b_query,
    b_value,
    w_out,
    b_out,
    ln1_gain,
    ln1_bias,
    w_up,
    b_up,
    w_down,
    b_down,
    ln2_gain,
    ln2_bias,
    out_grad_text,
    out_grad_roi,
):
    page_count, text_slots, width = text_emb.shape
    roi_slots = boxes.shape[1]
    slots = text_slots + roi_slots
    channels = feature_maps.shape[2]
    head_size = width // HEADS
    scale = head_size ** (-0.5)
    coarse_cells = COARSE * COARSE
    rows = page_count * slots
    dp_size = lax.axis_size("dp")
    mod_size = lax.axis_size("mod")
    top_bit = mod_size.bit_length() - 2
    my_mod = lax.axis_index("mod")
    bf16 = jnp.bfloat16
    f32 = jnp.float32

    vectors = (
        bn_gain,
        bn_bias,
        b_query,
        b_value,
        b_out,
        ln1_gain,
        ln1_bias,
        b_down,
        ln2_gain,
        ln2_bias,
        b_up,
    )
    vector_len = sum(vector.shape[0] for vector in vectors)
    matrix_rows = w_roi.shape[0] + 4 * w_query.shape[0]
    quantum = 16 * mod_size
    vector_rows = -(-(matrix_rows + -(-vector_len // width)) // quantum) * quantum - matrix_rows
    packed_vectors = jnp.pad(
        jnp.concatenate(vectors), (0, vector_rows * width - vector_len)
    ).reshape(vector_rows, width)
    pieces = (w_roi, w_query, w_key, w_value, w_out, packed_vectors)
    first_full = gather_all(jnp.concatenate(pieces, 0))
    ff_parts = w_up.shape[1] // width
    up_blocks = w_up.reshape(w_up.shape[0], ff_parts, width).transpose(1, 0, 2)
    second_full = gather_all(
        jnp.concatenate([up_blocks.reshape(-1, width), w_down], 0)
    )

    far_maps, far_boxes, far_grad = swapped(
        (feature_maps, boxes, out_grad_roi), "mod", top_bit
    )
    counts = lax.dynamic_slice_in_dim(row_counts, my_mod * page_count, page_count, 0)
    text_live = jnp.arange(text_slots, dtype=jnp.int32)[None, :] < counts[:, 0:1]
    roi_live = jnp.arange(roi_slots, dtype=jnp.int32)[None, :] < counts[:, 1:2]
    live = jnp.concatenate([text_live, roi_live], 1).reshape(rows, 1).astype(f32)
    roi_mask = roi_live.reshape(-1, 1).astype(f32)

    def pooled_part(mask, maps, area):
        return (
            jnp.einsum("prc,pcf->prf", mask.astype(bf16), maps, preferred_element_type=f32) / area
        )

    coarse_in, fine_in, coarse_area, fine_area = box_masks(far_boxes)
    pooled = (
        jnp.concatenate(
            [
                pooled_part(coarse_in, far_maps[:, :coarse_cells], coarse_area),
                pooled_part(fine_in, far_maps[:, coarse_cells:], fine_area),
            ],
            -1,
        )
        .astype(bf16)
        .reshape(page_count * roi_slots, 2 * channels)
    )

    starts = []
    at = 0
    for piece in pieces:
        starts.append(at)
        at += piece.shape[0]

    def unpack(full, start, count):
        return full[:, start : start + count].reshape(dp_size * count, width)

    roi_weight, query_weight, key_weight, value_weight, out_weight = (
        unpack(first_full, start, piece.shape[0]) for start, piece in zip(starts[:5], pieces[:5])
    )
    flat_vectors = first_full[:, starts[5] :].reshape(dp_size, vector_rows * width)
    full_vectors = []
    at = 0
    for vector in vectors:
        full_vectors.append(
            flat_vectors[:, at : at + vector.shape[0]].reshape(-1).astype(f32)
        )
        at += vector.shape[0]
    (
        norm_gain,
        norm_bias,
        query_bias,
        value_bias,
        out_bias,
        first_gain,
        first_bias,
        down_bias,
        second_gain,
        second_bias,
        up_bias,
    ) = full_vectors
    up_rows = w_up.shape[0] * ff_parts
    up_weight = (
        second_full[:, :up_rows]
        .reshape(dp_size, ff_parts, w_up.shape[0], width)
        .transpose(0, 2, 1, 3)
        .reshape(width, ff_parts * width)
    )
    down_weight = unpack(second_full, up_rows, w_down.shape[0])

    projected = product(pooled, roi_weight)
    stats = jnp.stack(
        [
            jnp.sum(projected * roi_mask, 0),
            jnp.sum(projected * projected * roi_mask, 0),
            jnp.broadcast_to(jnp.sum(roi_mask), (width,)),
        ]
    )
    stats = total_sum(stats)
    number = stats[2:3]
    average = stats[0:1] / number
    variance = stats[1:2] / number - average * average
    inv_std = lax.rsqrt(variance + 1e-05)
    standard = (projected - average) * inv_std
    roi_rows = (standard * norm_gain + norm_bias).astype(bf16)
    rows_in = jnp.concatenate(
        [text_emb, roi_rows.reshape(page_count, roi_slots, width)], 1
    ).reshape(rows, width)
    queries = (product(rows_in, query_weight) + query_bias).astype(bf16)
    keys = product(rows_in, key_weight).astype(bf16)
    values = (product(rows_in, value_weight) + value_bias).astype(bf16)
    attention_flops = 4 * rows * slots * width
    context, logs = attention_call(
        functools.partial(attend_kernel, text_slots, scale),
        counts,
        (queries, keys, values),
        (bf16, f32),
        page_count,
        attention_flops,
    )
    first_in = rows_in.astype(f32) + product(context, out_weight) + out_bias
    normed, first_average, first_inverse = norm_forward(first_in, first_gain, first_bias)
    normed_low = normed.astype(bf16)
    hidden = product(normed_low, up_weight) + up_bias
    cumulative = 0.5 * (1.0 + lax.erf(hidden * (0.5**0.5)))
    activated = (hidden * cumulative).astype(bf16)
    slope = (
        cumulative + hidden * (jnp.exp(-0.5 * hidden * hidden) * 0.3989422804014327)
    ).astype(bf16)
    second_in = normed + product(activated, down_weight) + down_bias
    normed_out, second_average, second_inverse = norm_forward(
        second_in, second_gain, second_bias
    )
    output = (normed_out * live).astype(bf16).reshape(page_count, slots, width)
    out_text = output[:, :text_slots]
    out_roi = swapped(output[:, text_slots:], "mod", top_bit)

    upstream = (
        jnp.concatenate([out_grad_text, far_grad], 1).reshape(rows, width).astype(f32) * live
    )
    grad_second, grad_ln2_gain, grad_ln2_bias = norm_backward(
        upstream, second_in, second_average, second_inverse, second_gain
    )
    grad_mixed = grad_second.astype(bf16)
    grad_w_down = inner_rows(activated, grad_mixed).astype(bf16)
    grad_b_down = jnp.sum(grad_mixed.astype(f32), 0)
    grad_hidden = (outer_cols(grad_mixed, down_weight) * slope.astype(f32)).astype(bf16)
    grad_w_up = inner_rows(normed_low, grad_hidden).astype(bf16)
    grad_b_up = jnp.sum(grad_hidden.astype(f32), 0)
    up_stack = (
        grad_w_up.reshape(dp_size, w_up.shape[0], ff_parts, width)
        .transpose(0, 2, 1, 3)
        .reshape(dp_size, up_rows, width)
    )
    second_share = scatter_sum(
        jnp.concatenate([up_stack, grad_w_down.reshape(dp_size, -1, width)], 1)
    )
    grad_first, grad_ln1_gain, grad_ln1_bias = norm_backward(
        grad_second + outer_cols(grad_hidden, up_weight),
        first_in,
        first_average,
        first_inverse,
        first_gain,
    )
    grad_attended = grad_first.astype(bf16)
    grad_w_out = inner_rows(context, grad_attended).astype(bf16)
    grad_b_out = jnp.sum(grad_attended.astype(f32), 0)
    grad_context = outer_cols(grad_attended, out_weight).astype(bf16)
    grad_queries, grad_keys, grad_values = attention_call(
        functools.partial(attend_back_kernel, text_slots, scale),
        counts,
        (queries, keys, values, grad_context, logs),
        (bf16, bf16, bf16),
        page_count,
        attention_flops * 5 // 2,
    )
    grad_rows = (
        grad_first
        + outer_cols(grad_queries, query_weight)
        + outer_cols(grad_keys, key_weight)
        + outer_cols(grad_values, value_weight)
    ).reshape(page_count, slots, width)
    grad_text = grad_rows[:, :text_slots]
    grad_roi = grad_rows[:, text_slots:].reshape(page_count * roi_slots, width)
    sums = total_sum(jnp.stack([jnp.sum(grad_roi, 0), jnp.sum(grad_roi * standard, 0)]))
    grad_w_query = inner_rows(rows_in, grad_queries).astype(bf16)
    grad_b_query = jnp.sum(grad_queries.astype(f32), 0)
    grad_w_key = inner_rows(rows_in, grad_keys).astype(bf16)
    grad_w_value = inner_rows(rows_in, grad_values).astype(bf16)
    grad_b_value = jnp.sum(grad_values.astype(f32), 0)
    sum_grad = sums[0:1]
    sum_scaled = sums[1:2]
    grad_projected = (
        inv_std
        * (
            grad_roi * norm_gain
            - roi_mask * norm_gain * (sum_grad + standard * sum_scaled) / number
        )
    ).astype(bf16)
    grad_w_roi = inner_rows(pooled, grad_projected).astype(bf16)
    grad_pooled = (
        outer_cols(grad_projected, roi_weight)
        .astype(bf16)
        .reshape(page_count, roi_slots, 2 * channels)
    )
    own_pooled = swapped(grad_pooled, "mod", top_bit)
    own_coarse, own_fine, own_coarse_area, own_fine_area = box_masks(boxes)

    def spread(mask, grad, area):
        return jnp.einsum(
            "prc,prf->pcf",
            mask.astype(bf16),
            (grad.astype(f32) / area).astype(bf16),
            preferred_element_type=f32,
        )

    grad_maps = jnp.concatenate(
        [
            spread(own_coarse, own_pooled[..., :channels], own_coarse_area),
            spread(own_fine, own_pooled[..., channels:], own_fine_area),
        ],
        1,
    )

    grad_vectors = (
        jnp.zeros_like(grad_b_out),
        jnp.zeros_like(grad_b_out),
        grad_b_query,
        grad_b_value,
        grad_b_out,
        grad_ln1_gain,
        grad_ln1_bias,
        grad_b_down,
        grad_ln2_gain,
        grad_ln2_bias,
        grad_b_up,
    )
    vector_stack = jnp.concatenate(
        [vector.astype(bf16).reshape(dp_size, -1) for vector in grad_vectors], 1
    )
    vector_stack = jnp.pad(
        vector_stack, ((0, 0), (0, vector_rows * width - vector_len))
    ).reshape(dp_size, vector_rows, width)
    first_share = scatter_sum(
        jnp.concatenate(
            [
                grad.reshape(dp_size, -1, width)
                for grad in (grad_w_roi, grad_w_query, grad_w_key, grad_w_value, grad_w_out)
            ]
            + [vector_stack],
            1,
        )
    ).astype(f32)
    own_w_roi, own_w_query, own_w_key, own_w_value, own_w_out = (
        first_share[start : start + piece.shape[0]]
        for start, piece in zip(starts[:5], pieces[:5])
    )
    flat_share = first_share[starts[5] :].reshape(-1)
    vector_shares = []
    at = 0
    for vector in vectors:
        vector_shares.append(flat_share[at : at + vector.shape[0]])
        at += vector.shape[0]
    own_w_up = (
        second_share[:up_rows]
        .reshape(ff_parts, w_up.shape[0], width)
        .transpose(1, 0, 2)
        .reshape(w_up.shape)
        .astype(f32)
    )
    own_w_down = second_share[up_rows:].astype(f32)
    share_len = width // dp_size
    share_start = lax.axis_index("dp") * share_len
    gain_share = lax.dynamic_slice_in_dim(sums[1], share_start, share_len, 0)
    bias_share = lax.dynamic_slice_in_dim(sums[0], share_start, share_len, 0)
    return (
        out_text,
        out_roi,
        grad_text,
        grad_maps,
        own_w_roi,
        gain_share,
        bias_share,
        own_w_query,
        own_w_key,
        own_w_value,
        vector_shares[2],
        vector_shares[3],
        own_w_out,
        vector_shares[4],
        vector_shares[5],
        vector_shares[6],
        own_w_up,
        vector_shares[10],
        own_w_down,
        vector_shares[7],
        vector_shares[8],
        vector_shares[9],
    )


def solution(mesh):
    in_specs = (
        P(("dp", "mod"), None, None),
        P(("dp", "mod"), None, None),
        P(("dp", "mod"), None, None),
        P("dp", None),
        P("dp", None),
        P("dp"),
        P("dp"),
        P("dp", None),
        P("dp", None),
        P("dp", None),
        P("dp"),
        P("dp"),
        P("dp", None),
        P("dp"),
        P("dp"),
        P("dp"),
        P("dp", None),
        P("dp"),
        P("dp", None),
        P("dp"),
        P("dp"),
        P("dp"),
        P(("dp", "mod"), None, None),
        P(("dp", "mod"), None, None),
    )
    out_specs = (
        P(("dp", "mod"), None, None),
        P(("dp", "mod"), None, None),
        P(("dp", "mod"), None, None),
        P(("dp", "mod"), None, None),
        P("dp", None),
        P("dp"),
        P("dp"),
        P("dp", None),
        P("dp", None),
        P("dp", None),
        P("dp"),
        P("dp"),
        P("dp", None),
        P("dp"),
        P("dp"),
        P("dp"),
        P("dp", None),
        P("dp"),
        P("dp", None),
        P("dp"),
        P("dp"),
        P("dp"),
    )
    return jax.shard_map(body, mesh=mesh, in_specs=in_specs, out_specs=out_specs, check_vma=False)
```

```python
import functools

import jax
import jax.numpy as jnp
from jax import lax
from jax.experimental import pallas as pl
from jax.experimental.pallas import tpu as pltpu
from jax.sharding import PartitionSpec as P

HEADS = 12
FINE = 16
COARSE = 8
PAIR = 128
BOTH = ("dp", "mod")


def swapped(block, axis, distance):
    count = lax.axis_size(axis)
    route = []
    for low in range(count):
        high = low | 1 << distance
        if high != low and high < count:
            route += [(low, high), (high, low)]
    return lax.ppermute(block, axis, route)


def product(left_mat, right_mat):
    return jnp.dot(left_mat, right_mat, preferred_element_type=jnp.float32)


def inner_rows(left_mat, right_mat):
    return lax.dot_general(
        left_mat, right_mat, (((0,), (0,)), ((), ())), preferred_element_type=jnp.float32
    )


def outer_cols(left_mat, right_mat):
    return lax.dot_general(
        left_mat, right_mat, (((1,), (1,)), ((), ())), preferred_element_type=jnp.float32
    )


def norm_forward(hidden_in, gain_vec, bias_vec):
    average = jnp.mean(hidden_in, axis=-1, keepdims=True)
    centered = hidden_in - average
    variance = jnp.mean(centered * centered, axis=-1, keepdims=True)
    inverse = lax.rsqrt(variance + 1e-05)
    return centered * inverse * gain_vec + bias_vec, average, inverse


def norm_backward(grad_out, hidden_in, average, inverse, gain_vec):
    standard = (hidden_in - average) * inverse
    grad_gain = jnp.sum(grad_out * standard, 0)
    grad_bias = jnp.sum(grad_out, 0)
    scaled = grad_out * gain_vec
    mean_scaled = jnp.mean(scaled, axis=-1, keepdims=True)
    mean_cross = jnp.mean(scaled * standard, axis=-1, keepdims=True)
    grad_hidden = inverse * (scaled - mean_scaled - standard * mean_cross)
    return grad_hidden, grad_gain, grad_bias


def box_masks(boxes):
    left_edge = boxes[..., 0:1]
    top_edge = boxes[..., 1:2]
    right_edge = boxes[..., 2:3]
    bottom_edge = boxes[..., 3:4]
    fine_cell = jnp.arange(FINE * FINE, dtype=jnp.int32)
    fine_row = fine_cell // FINE
    fine_col = fine_cell % FINE
    inside_fine = (
        (fine_col >= left_edge)
        & (fine_col < right_edge)
        & (fine_row >= top_edge)
        & (fine_row < bottom_edge)
    )
    coarse_cell = jnp.arange(COARSE * COARSE, dtype=jnp.int32)
    coarse_row = coarse_cell // COARSE
    coarse_col = coarse_cell % COARSE
    inside_coarse = (
        (coarse_col >= left_edge // 2)
        & (coarse_col < (right_edge + 1) // 2)
        & (coarse_row >= top_edge // 2)
        & (coarse_row < (bottom_edge + 1) // 2)
    )
    coarse_area = jnp.sum(inside_coarse.astype(jnp.float32), -1, keepdims=True)
    fine_area = jnp.sum(inside_fine.astype(jnp.float32), -1, keepdims=True)
    return inside_coarse, inside_fine, coarse_area, fine_area


def key_live(counts_ref, page, text_slots, slots):
    col = lax.broadcasted_iota(jnp.int32, (1, slots), 1)
    text_count = counts_ref[page, 0]
    roi_count = counts_ref[page, 1]
    return (col < text_count) | ((col >= text_slots) & (col < text_slots + roi_count))


def attend_kernel(text_slots, scale, counts_ref, query_ref, key_ref, value_ref, out_ref, log_ref):
    slots = query_ref.shape[0]
    live = key_live(counts_ref, pl.program_id(0), text_slots, slots)
    lane = lax.broadcasted_iota(jnp.int32, (1, PAIR), 1)
    query = query_ref[...] * scale
    keys = key_ref[...]
    values = value_ref[...]
    parts = []
    logs = []
    for head in range(2):
        mine = (lane // (PAIR // 2)) == head
        masked = jnp.where(mine, query, jnp.zeros_like(query))
        scores = jnp.where(live, outer_cols(masked, keys), -1e30)
        highest = jnp.max(scores, -1, keepdims=True)
        exponent = jnp.exp(scores - highest)
        total = jnp.sum(exponent, -1, keepdims=True)
        weights = (exponent * (1.0 / total)).astype(jnp.bfloat16)
        parts.append(product(weights, values))
        logs.append(highest + jnp.log(total))
    first = lane < PAIR // 2
    out_ref[...] = jnp.where(first, parts[0], parts[1]).astype(jnp.bfloat16)
    log_ref[...] = jnp.where(first, logs[0], logs[1])


def attend_back_kernel(
    text_slots,
    scale,
    counts_ref,
    query_ref,
    key_ref,
    value_ref,
    grad_ref,
    log_ref,
    grad_query_ref,
    grad_key_ref,
    grad_value_ref,
):
    slots = query_ref.shape[0]
    live = key_live(counts_ref, pl.program_id(0), text_slots, slots)
    lane = lax.broadcasted_iota(jnp.int32, (1, PAIR), 1)
    query = query_ref[...] * scale
    keys = key_ref[...]
    values = value_ref[...]
    grad = grad_ref[...]
    logs = log_ref[...]
    queries_out = []
    keys_out = []
    values_out = []
    for head in range(2):
        mine = (lane // (PAIR // 2)) == head
        masked = jnp.where(mine, query, jnp.zeros_like(query))
        grad_mine = jnp.where(mine, grad, jnp.zeros_like(grad))
        log_col = logs[:, head * (PAIR // 2) : head * (PAIR // 2) + 1]
        weights = jnp.exp(jnp.where(live, outer_cols(masked, keys), -1e30) - log_col)
        grad_weights = outer_cols(grad_mine, values)
        delta = jnp.sum(grad_weights * weights, -1, keepdims=True)
        grad_scores = (weights * (grad_weights - delta)).astype(jnp.bfloat16)
        values_out.append(inner_rows(weights.astype(jnp.bfloat16), grad))
        queries_out.append(product(grad_scores, keys))
        keys_out.append(inner_rows(grad_scores, query))
    first = lane < PAIR // 2
    grad_query_ref[...] = (jnp.where(first, queries_out[0], queries_out[1]) * scale).astype(
        jnp.bfloat16
    )
    grad_key_ref[...] = jnp.where(first, keys_out[0], keys_out[1]).astype(jnp.bfloat16)
    grad_value_ref[...] = jnp.where(first, values_out[0], values_out[1]).astype(jnp.bfloat16)


def attention_call(kernel, counts, operands, out_types, page_count, flops):
    rows, width = operands[0].shape
    slots = rows // page_count
    spec = pl.BlockSpec((slots, PAIR), lambda page, pair, counts_ref: (page, pair))
    return pl.pallas_call(
        kernel,
        out_shape=tuple(jax.ShapeDtypeStruct((rows, width), kind) for kind in out_types),
        grid_spec=pltpu.PrefetchScalarGridSpec(
            num_scalar_prefetch=1,
            grid=(page_count, width // PAIR),
            in_specs=[spec] * len(operands),
            out_specs=tuple([spec] * len(out_types)),
        ),
        cost_estimate=pl.CostEstimate(
            flops=flops,
            bytes_accessed=rows * width * 2 * (len(operands) + len(out_types)),
            transcendentals=rows * slots * HEADS,
        ),
        compiler_params=pltpu.CompilerParams(
            dimension_semantics=("arbitrary", "arbitrary"), vmem_limit_bytes=40 << 20
        ),
    )(counts, *operands)


def gather_all(shard):
    mod_size = lax.axis_size("mod")
    piece = shard.shape[0] // mod_size
    mine = lax.dynamic_slice_in_dim(shard, lax.axis_index("mod") * piece, piece, 0)
    full = lax.all_gather(mine, BOTH, axis=0, tiled=True)
    return full.reshape(-1, *shard.shape)


def scatter_sum(stacked):
    dp_size, rows, width = stacked.shape
    part = lax.psum_scatter(
        stacked.reshape(dp_size * rows, width), BOTH, scatter_dimension=0, tiled=True
    )
    return lax.all_gather(part, "mod", axis=0, tiled=True)


MESH = pl.DeviceIdType.MESH


def grid_sizes():
    dp_size = lax.axis_size("dp")
    mod_size = lax.axis_size("mod")
    short = 1 << ((dp_size.bit_length() - 1) // 2)
    return dp_size // short, short, mod_size // 2


def place(sizes):
    _, short, _ = sizes
    dp_index = lax.axis_index("dp")
    mod_index = lax.axis_index("mod")
    return dp_index // short, dp_index % short, mod_index // 2, mod_index % 2


def device_at(sizes, row, col, wide, core):
    return {"dp": row * sizes[1] + col, "mod": wide * 2 + core}


def greet(peers):
    barrier = pltpu.get_barrier_semaphore()
    for peer in peers:
        pl.semaphore_signal(barrier, inc=1, device_id=peer, device_id_type=MESH)
    pl.semaphore_wait(barrier, len(peers))


def send(source, target, send_sem, recv_sem, peer):
    copy = pltpu.make_async_remote_copy(
        src_ref=source,
        dst_ref=target,
        send_sem=send_sem,
        recv_sem=recv_sem,
        device_id=peer,
        device_id_type=MESH,
    )
    copy.start()
    return copy


def total_kernel(mod_size, dp_size, stats_ref, out_ref, near, far, send_sem, recv_sem):
    my_mod = lax.axis_index("mod")
    my_dp = lax.axis_index("dp")
    near_peers = [{"mod": (my_mod + step) % mod_size} for step in range(1, mod_size)]
    far_peers = [{"dp": (my_dp + step) % dp_size} for step in range(1, dp_size)]
    greet(near_peers + far_peers)
    near[my_mod] = stats_ref[...]
    copies = [
        send(stats_ref, near.at[my_mod], send_sem.at[at], recv_sem.at[at], peer)
        for at, peer in enumerate(near_peers)
    ]
    for copy in copies:
        copy.wait()
    group = near[0]
    for at in range(1, mod_size):
        group = group + near[at]
    far[my_dp] = group
    copies = [
        send(
            far.at[my_dp],
            far.at[my_dp],
            send_sem.at[mod_size - 1 + at],
            recv_sem.at[mod_size - 1 + at],
            peer,
        )
        for at, peer in enumerate(far_peers)
    ]
    for copy in copies:
        copy.wait()
    total = far[0]
    for at in range(1, dp_size):
        total = total + far[at]
    out_ref[...] = total


def total_sum(stats, call_id):
    mod_size = lax.axis_size("mod")
    dp_size = lax.axis_size("dp")
    messages = mod_size + dp_size - 2
    padded = jnp.pad(stats, ((0, -stats.shape[0] % 8), (0, 0)))
    vmem = pl.BlockSpec(memory_space=pltpu.VMEM)
    return pl.pallas_call(
        functools.partial(total_kernel, mod_size, dp_size),
        out_shape=jax.ShapeDtypeStruct(padded.shape, jnp.float32),
        in_specs=[vmem],
        out_specs=vmem,
        scratch_shapes=[
            pltpu.VMEM((mod_size, *padded.shape), jnp.float32),
            pltpu.VMEM((dp_size, *padded.shape), jnp.float32),
            pltpu.SemaphoreType.DMA((messages,)),
            pltpu.SemaphoreType.DMA((messages,)),
        ],
        compiler_params=pltpu.CompilerParams(
            collective_id=call_id, has_side_effects=True, vmem_limit_bytes=8 << 20
        ),
        name=f"total_{call_id}",
    )(padded)


def gather_kernel(sizes, shard_ref, out_ref, send_sem, recv_sem, local_sem):
    rows, cols, wides = sizes
    row, col, wide, core = place(sizes)
    row_peers = [((row + step) % rows, col, wide, core) for step in range(1, rows)]
    col_peers = [(row, (col + step) % cols, wide, core) for step in range(1, cols)]
    wide_peers = [(row, col, (wide + step) % wides, core) for step in range(1, wides)]
    partner = (row, col, wide, 1 - core)
    own = pltpu.make_async_copy(shard_ref, out_ref.at[row, col], local_sem)
    own.start()
    own.wait()
    greet(
        [device_at(sizes, *peer) for peer in row_peers + col_peers + wide_peers + [partner]]
    )
    used = [0]
    pending = []

    def push(source, target, peer):
        at = used[0]
        used[0] += 1
        return send(
            source, target, send_sem.at[at], recv_sem.at[at], device_at(sizes, *peer)
        )

    def arrive(copies):
        for copy in copies:
            copy.wait_recv()
        pending.extend(copies)

    split_rows = [
        push(shard_ref.at[core, 0, wide], out_ref.at[row, col, core, 0, wide], peer)
        for peer in row_peers
    ]
    whole_rows = [
        push(shard_ref.at[core, 1], out_ref.at[row, col, core, 1], peer) for peer in row_peers
    ]
    arrive(split_rows)
    view = out_ref.at[:, col, core, 0, wide]
    split_cols = [push(view, view, peer) for peer in col_peers]
    arrive(whole_rows)
    view = out_ref.at[:, col, core, 1]
    whole_cols = [push(view, view, peer) for peer in col_peers]
    arrive(split_cols)
    view = out_ref.at[:, :, core, 0, wide]
    split_wide = [push(view, view, peer) for peer in wide_peers]
    arrive(whole_cols)
    view = out_ref.at[:, :, core, 1]
    whole_core = [push(view, view, partner)]
    arrive(split_wide)
    view = out_ref.at[:, :, core, 0]
    split_core = [push(view, view, partner)]
    arrive(whole_core)
    arrive(split_core)
    for copy in pending:
        copy.wait_send()


def quick_gather(shard, call_id):
    sizes = grid_sizes()
    rows, cols, wides = sizes
    height, width = shard.shape
    part = height // (4 * wides)
    messages = 2 * (rows - 1) + 2 * (cols - 1) + (wides - 1) + 2
    vmem = pl.BlockSpec(memory_space=pltpu.VMEM)
    out = pl.pallas_call(
        functools.partial(gather_kernel, sizes),
        out_shape=jax.ShapeDtypeStruct((rows, cols, 2, 2, wides, part, width), shard.dtype),
        in_specs=[vmem],
        out_specs=vmem,
        scratch_shapes=[
            pltpu.SemaphoreType.DMA((messages,)),
            pltpu.SemaphoreType.DMA((messages,)),
            pltpu.SemaphoreType.DMA(()),
        ],
        compiler_params=pltpu.CompilerParams(
            collective_id=call_id, has_side_effects=True, vmem_limit_bytes=32 << 20
        ),
        name="gather_weights",
    )(shard.reshape(2, 2, wides, part, width))
    return out.reshape(rows * cols, height, width)


def add_into(target, base, extras):
    total = base.astype(jnp.float32)
    for extra in extras:
        total = total + extra.astype(jnp.float32)
    target[...] = total.astype(target.dtype)


def scatter_kernel(
    sizes,
    grad_ref,
    out_ref,
    core_in,
    core_sum,
    col_in,
    col_sum,
    row_in,
    row_sum,
    wide_in,
    other_wide_in,
    other_wide_sum,
    other_col_in,
    other_col_sum,
    other_row_in,
    send_sem,
    recv_sem,
):
    rows, cols, wides = sizes
    row, col, wide, core = place(sizes)
    row_peers = [((row + step) % rows, col, wide, core) for step in range(1, rows)]
    col_peers = [(row, (col + step) % cols, wide, core) for step in range(1, cols)]
    wide_peers = [(row, col, (wide + step) % wides, core) for step in range(1, wides)]
    cross_peers = [(row, col, (wide + step) % wides, 1 - core) for step in range(wides)]
    partner = cross_peers[0]
    greet(
        [device_at(sizes, *peer) for peer in row_peers + col_peers + wide_peers + cross_peers]
    )
    used = [0]
    pending = []

    def push(source, target, peer):
        at = used[0]
        used[0] += 1
        return send(
            source, target, send_sem.at[at], recv_sem.at[at], device_at(sizes, *peer)
        )

    def arrive(copies):
        for copy in copies:
            copy.wait_recv()
        pending.extend(copies)

    core_copies = [
        push(grad_ref.at[:, :, 1 - core, half], core_in.at[half], partner) for half in range(2)
    ]

    def fold_core(half):
        arrive([core_copies[half]])

        def step(at, carry):
            z = at // cols
            y = at % cols
            add_into(
                core_sum.at[half, z, y],
                grad_ref[z, y, core, half],
                [core_in[half, z, y]],
            )
            return carry

        lax.fori_loop(0, rows * cols, step, 0)

    fold_core(0)
    col_copies = [
        push(core_sum.at[0, :, peer[1]], col_in.at[at], peer) for at, peer in enumerate(col_peers)
    ]
    fold_core(1)
    other_wide_copies = [
        push(core_sum.at[1, :, :, peer[2]], other_wide_in.at[at], peer)
        for at, peer in enumerate(wide_peers)
    ]
    arrive(col_copies)

    def fold_col(z, carry):
        add_into(
            col_sum.at[z], core_sum[0, z, col], [col_in[at, z] for at in range(cols - 1)]
        )
        return carry

    lax.fori_loop(0, rows, fold_col, 0)
    row_copies = [
        push(col_sum.at[peer[0]], row_in.at[at], peer) for at, peer in enumerate(row_peers)
    ]
    arrive(other_wide_copies)

    def fold_other_wide(at, carry):
        z = at // cols
        y = at % cols
        add_into(
            other_wide_sum.at[z, y],
            core_sum[1, z, y, wide],
            [other_wide_in[peer, z, y] for peer in range(wides - 1)],
        )
        return carry

    lax.fori_loop(0, rows * cols, fold_other_wide, 0)
    other_col_copies = [
        push(other_wide_sum.at[:, peer[1]], other_col_in.at[at], peer)
        for at, peer in enumerate(col_peers)
    ]
    arrive(other_col_copies)

    def fold_other_col(z, carry):
        add_into(
            other_col_sum.at[z],
            other_wide_sum[z, col],
            [other_col_in[at, z] for at in range(cols - 1)],
        )
        return carry

    lax.fori_loop(0, rows, fold_other_col, 0)
    other_row_copies = [
        push(other_col_sum.at[peer[0]], other_row_in.at[at], peer)
        for at, peer in enumerate(row_peers)
    ]
    arrive(row_copies)
    add_into(row_sum, col_sum[row], [row_in[at] for at in range(rows - 1)])
    wide_copies = [
        push(row_sum.at[peer[2]], wide_in.at[at], peer) for at, peer in enumerate(wide_peers)
    ]
    arrive(other_row_copies)
    add_into(
        out_ref.at[core, 1, wide],
        other_col_sum[row],
        [other_row_in[at] for at in range(rows - 1)],
    )
    last = [
        push(out_ref.at[core, 1, wide], out_ref.at[core, 1, wide], peer)
        for peer in wide_peers + cross_peers
    ]
    arrive(wide_copies)
    add_into(
        out_ref.at[core, 0, wide], row_sum[wide], [wide_in[at] for at in range(wides - 1)]
    )
    last += [
        push(out_ref.at[core, 0, wide], out_ref.at[core, 0, wide], peer)
        for peer in wide_peers + cross_peers
    ]
    arrive(last)
    for copy in pending:
        copy.wait_send()


def quick_scatter(stacked, call_id):
    sizes = grid_sizes()
    rows, cols, wides = sizes
    _, height, width = stacked.shape
    part = height // (4 * wides)
    messages = (
        2 + 2 * (cols - 1) + 2 * (wides - 1) + 2 * (rows - 1) + 2 * (2 * wides - 1)
    )
    vmem = pl.BlockSpec(memory_space=pltpu.VMEM)
    kind = stacked.dtype

    def buffer(*shape):
        return pltpu.VMEM((*shape, part, width), kind)

    out = pl.pallas_call(
        functools.partial(scatter_kernel, sizes),
        out_shape=jax.ShapeDtypeStruct((2, 2, wides, part, width), kind),
        in_specs=[vmem],
        out_specs=vmem,
        scratch_shapes=[
            buffer(2, rows, cols, wides),
            buffer(2, rows, cols, wides),
            buffer(cols - 1, rows, wides),
            buffer(rows, wides),
            buffer(rows - 1, wides),
            buffer(wides),
            buffer(wides - 1),
            buffer(wides - 1, rows, cols),
            buffer(rows, cols),
            buffer(cols - 1, rows),
            buffer(rows),
            buffer(rows - 1),
            pltpu.SemaphoreType.DMA((messages,)),
            pltpu.SemaphoreType.DMA((messages,)),
        ],
        compiler_params=pltpu.CompilerParams(
            collective_id=call_id, has_side_effects=True, vmem_limit_bytes=56 << 20
        ),
        name="scatter_grads",
    )(stacked.reshape(rows, cols, 2, 2, wides, part, width))
    return out.reshape(height, width)


def body(
    text_emb,
    feature_maps,
    boxes,
    row_counts,
    w_roi,
    bn_gain,
    bn_bias,
    w_query,
    w_key,
    w_value,
    b_query,
    b_value,
    w_out,
    b_out,
    ln1_gain,
    ln1_bias,
    w_up,
    b_up,
    w_down,
    b_down,
    ln2_gain,
    ln2_bias,
    out_grad_text,
    out_grad_roi,
):
    page_count, text_slots, width = text_emb.shape
    roi_slots = boxes.shape[1]
    slots = text_slots + roi_slots
    channels = feature_maps.shape[2]
    head_size = width // HEADS
    scale = head_size ** (-0.5)
    coarse_cells = COARSE * COARSE
    rows = page_count * slots
    dp_size = lax.axis_size("dp")
    mod_size = lax.axis_size("mod")
    top_bit = mod_size.bit_length() - 2
    my_mod = lax.axis_index("mod")
    bf16 = jnp.bfloat16
    f32 = jnp.float32

    vectors = (
        bn_gain,
        bn_bias,
        b_query,
        b_value,
        b_out,
        ln1_gain,
        ln1_bias,
        b_down,
        ln2_gain,
        ln2_bias,
        b_up,
    )
    vector_len = sum(vector.shape[0] for vector in vectors)
    pieces = (w_roi, w_query, w_key, w_value)
    matrix_rows = sum(piece.shape[0] for piece in pieces)
    quantum = 32 * mod_size
    vector_rows = -(-(matrix_rows + -(-vector_len // width)) // quantum) * quantum - matrix_rows
    packed_vectors = jnp.pad(
        jnp.concatenate(vectors), (0, vector_rows * width - vector_len)
    ).reshape(vector_rows, width)
    first_full = quick_gather(jnp.concatenate([*pieces, packed_vectors], 0), 1)
    ff_parts = w_up.shape[1] // width
    up_blocks = w_up.reshape(w_up.shape[0], ff_parts, width).transpose(1, 0, 2)
    second_full = gather_all(
        jnp.concatenate([up_blocks.reshape(-1, width), w_down, w_out], 0)
    )

    far_maps, far_boxes, far_grad = swapped(
        (feature_maps, boxes, out_grad_roi), "mod", top_bit
    )
    counts = lax.dynamic_slice_in_dim(row_counts, my_mod * page_count, page_count, 0)
    text_live = jnp.arange(text_slots, dtype=jnp.int32)[None, :] < counts[:, 0:1]
    roi_live = jnp.arange(roi_slots, dtype=jnp.int32)[None, :] < counts[:, 1:2]
    live = jnp.concatenate([text_live, roi_live], 1).reshape(rows, 1).astype(f32)
    roi_mask = roi_live.reshape(-1, 1).astype(f32)

    def pooled_part(mask, maps, area):
        return (
            jnp.einsum("prc,pcf->prf", mask.astype(bf16), maps, preferred_element_type=f32) / area
        )

    coarse_in, fine_in, coarse_area, fine_area = box_masks(far_boxes)
    pooled = (
        jnp.concatenate(
            [
                pooled_part(coarse_in, far_maps[:, :coarse_cells], coarse_area),
                pooled_part(fine_in, far_maps[:, coarse_cells:], fine_area),
            ],
            -1,
        )
        .astype(bf16)
        .reshape(page_count * roi_slots, 2 * channels)
    )

    starts = []
    at = 0
    for piece in pieces:
        starts.append(at)
        at += piece.shape[0]

    def unpack(full, start, count):
        return full[:, start : start + count].reshape(dp_size * count, width)

    roi_weight, query_weight, key_weight, value_weight = (
        unpack(first_full, start, piece.shape[0]) for start, piece in zip(starts, pieces)
    )
    flat_vectors = first_full[:, matrix_rows:].reshape(dp_size, vector_rows * width)
    full_vectors = []
    at = 0
    for vector in vectors:
        full_vectors.append(
            flat_vectors[:, at : at + vector.shape[0]].reshape(-1).astype(f32)
        )
        at += vector.shape[0]
    (
        norm_gain,
        norm_bias,
        query_bias,
        value_bias,
        out_bias,
        first_gain,
        first_bias,
        down_bias,
        second_gain,
        second_bias,
        up_bias,
    ) = full_vectors
    up_rows = w_up.shape[0] * ff_parts
    up_weight = (
        second_full[:, :up_rows]
        .reshape(dp_size, ff_parts, w_up.shape[0], width)
        .transpose(0, 2, 1, 3)
        .reshape(width, ff_parts * width)
    )
    down_weight = unpack(second_full, up_rows, w_down.shape[0])
    out_weight = unpack(second_full, up_rows + w_down.shape[0], w_out.shape[0])

    projected = product(pooled, roi_weight)
    stats = jnp.stack(
        [
            jnp.sum(projected * roi_mask, 0),
            jnp.sum(projected * projected * roi_mask, 0),
            jnp.broadcast_to(jnp.sum(roi_mask), (width,)),
        ]
    )
    stats = total_sum(stats, 2)
    number = stats[2:3]
    average = stats[0:1] / number
    variance = stats[1:2] / number - average * average
    inv_std = lax.rsqrt(variance + 1e-05)
    standard = (projected - average) * inv_std
    roi_rows = (standard * norm_gain + norm_bias).astype(bf16)
    rows_in = jnp.concatenate(
        [text_emb, roi_rows.reshape(page_count, roi_slots, width)], 1
    ).reshape(rows, width)
    queries = (product(rows_in, query_weight) + query_bias).astype(bf16)
    keys = product(rows_in, key_weight).astype(bf16)
    values = (product(rows_in, value_weight) + value_bias).astype(bf16)
    attention_flops = 4 * rows * slots * width
    context, logs = attention_call(
        functools.partial(attend_kernel, text_slots, scale),
        counts,
        (queries, keys, values),
        (bf16, f32),
        page_count,
        attention_flops,
    )
    first_in = rows_in.astype(f32) + product(context, out_weight) + out_bias
    normed, first_average, first_inverse = norm_forward(first_in, first_gain, first_bias)
    normed_low = normed.astype(bf16)
    hidden = product(normed_low, up_weight) + up_bias
    cumulative = 0.5 * (1.0 + lax.erf(hidden * (0.5**0.5)))
    activated = (hidden * cumulative).astype(bf16)
    slope = (
        cumulative + hidden * (jnp.exp(-0.5 * hidden * hidden) * 0.3989422804014327)
    ).astype(bf16)
    second_in = normed + product(activated, down_weight) + down_bias
    normed_out, second_average, second_inverse = norm_forward(
        second_in, second_gain, second_bias
    )
    output = (normed_out * live).astype(bf16).reshape(page_count, slots, width)
    out_text = output[:, :text_slots]
    out_roi = swapped(output[:, text_slots:], "mod", top_bit)

    upstream = (
        jnp.concatenate([out_grad_text, far_grad], 1).reshape(rows, width).astype(f32) * live
    )
    grad_second, grad_ln2_gain, grad_ln2_bias = norm_backward(
        upstream, second_in, second_average, second_inverse, second_gain
    )
    grad_mixed = grad_second.astype(bf16)
    grad_w_down = inner_rows(activated, grad_mixed).astype(bf16)
    grad_b_down = jnp.sum(grad_mixed.astype(f32), 0)
    grad_hidden = (outer_cols(grad_mixed, down_weight) * slope.astype(f32)).astype(bf16)
    grad_w_up = inner_rows(normed_low, grad_hidden).astype(bf16)
    grad_b_up = jnp.sum(grad_hidden.astype(f32), 0)
    up_stack = (
        grad_w_up.reshape(dp_size, w_up.shape[0], ff_parts, width)
        .transpose(0, 2, 1, 3)
        .reshape(dp_size, up_rows, width)
    )
    second_share = scatter_sum(
        jnp.concatenate([up_stack, grad_w_down.reshape(dp_size, -1, width)], 1)
    )
    grad_first, grad_ln1_gain, grad_ln1_bias = norm_backward(
        grad_second + outer_cols(grad_hidden, up_weight),
        first_in,
        first_average,
        first_inverse,
        first_gain,
    )
    grad_attended = grad_first.astype(bf16)
    grad_w_out = inner_rows(context, grad_attended).astype(bf16)
    grad_b_out = jnp.sum(grad_attended.astype(f32), 0)
    grad_context = outer_cols(grad_attended, out_weight).astype(bf16)
    grad_queries, grad_keys, grad_values = attention_call(
        functools.partial(attend_back_kernel, text_slots, scale),
        counts,
        (queries, keys, values, grad_context, logs),
        (bf16, bf16, bf16),
        page_count,
        attention_flops * 5 // 2,
    )
    grad_rows = (
        grad_first
        + outer_cols(grad_queries, query_weight)
        + outer_cols(grad_keys, key_weight)
        + outer_cols(grad_values, value_weight)
    ).reshape(page_count, slots, width)
    grad_text = grad_rows[:, :text_slots]
    grad_roi = grad_rows[:, text_slots:].reshape(page_count * roi_slots, width)
    grad_w_query = inner_rows(rows_in, grad_queries).astype(bf16)
    grad_b_query = jnp.sum(grad_queries.astype(f32), 0)
    grad_w_key = inner_rows(rows_in, grad_keys).astype(bf16)
    grad_w_value = inner_rows(rows_in, grad_values).astype(bf16)
    grad_b_value = jnp.sum(grad_values.astype(f32), 0)
    grad_vectors = (
        jnp.sum(grad_roi * standard, 0),
        jnp.sum(grad_roi, 0),
        grad_b_query,
        grad_b_value,
        grad_b_out,
        grad_ln1_gain,
        grad_ln1_bias,
        grad_b_down,
        grad_ln2_gain,
        grad_ln2_bias,
    )
    sums = total_sum(
        jnp.concatenate(
            [vector[None] for vector in grad_vectors] + [grad_b_up.reshape(ff_parts, width)], 0
        ),
        3,
    )
    sum_scaled = sums[0:1]
    sum_grad = sums[1:2]
    grad_projected = (
        inv_std
        * (
            grad_roi * norm_gain
            - roi_mask * norm_gain * (sum_grad + standard * sum_scaled) / number
        )
    ).astype(bf16)
    grad_w_roi = inner_rows(pooled, grad_projected).astype(bf16)
    grad_pooled = (
        outer_cols(grad_projected, roi_weight)
        .astype(bf16)
        .reshape(page_count, roi_slots, 2 * channels)
    )
    own_pooled = swapped(grad_pooled, "mod", top_bit)
    own_coarse, own_fine, own_coarse_area, own_fine_area = box_masks(boxes)

    def spread(mask, grad, area):
        return jnp.einsum(
            "prc,prf->pcf",
            mask.astype(bf16),
            (grad.astype(f32) / area).astype(bf16),
            preferred_element_type=f32,
        )

    grad_maps = jnp.concatenate(
        [
            spread(own_coarse, own_pooled[..., :channels], own_coarse_area),
            spread(own_fine, own_pooled[..., channels:], own_fine_area),
        ],
        1,
    )

    first_share = quick_scatter(
        jnp.concatenate(
            [
                grad.reshape(dp_size, -1, width)
                for grad in (grad_w_roi, grad_w_query, grad_w_key, grad_w_value, grad_w_out)
            ],
            1,
        ),
        4,
    ).astype(f32)
    own_matrices = []
    at = 0
    for piece in (*pieces, w_out):
        own_matrices.append(first_share[at : at + piece.shape[0]])
        at += piece.shape[0]
    own_w_roi, own_w_query, own_w_key, own_w_value, own_w_out = own_matrices
    own_w_up = (
        second_share[:up_rows]
        .reshape(ff_parts, w_up.shape[0], width)
        .transpose(1, 0, 2)
        .reshape(w_up.shape)
        .astype(f32)
    )
    own_w_down = second_share[up_rows:].astype(f32)
    my_dp = lax.axis_index("dp")
    share_len = width // dp_size
    vector_share = lax.dynamic_slice_in_dim(
        sums[: len(grad_vectors)], my_dp * share_len, share_len, 1
    )
    up_share = lax.dynamic_slice_in_dim(
        sums[len(grad_vectors) : len(grad_vectors) + ff_parts].reshape(-1),
        my_dp * b_up.shape[0],
        b_up.shape[0],
        0,
    )
    return (
        out_text,
        out_roi,
        grad_text,
        grad_maps,
        own_w_roi,
        vector_share[0],
        vector_share[1],
        own_w_query,
        own_w_key,
        own_w_value,
        vector_share[2],
        vector_share[3],
        own_w_out,
        vector_share[4],
        vector_share[5],
        vector_share[6],
        own_w_up,
        up_share,
        own_w_down,
        vector_share[7],
        vector_share[8],
        vector_share[9],
    )


def solution(mesh):
    in_specs = (
        P(("dp", "mod"), None, None),
        P(("dp", "mod"), None, None),
        P(("dp", "mod"), None, None),
        P("dp", None),
        P("dp", None),
        P("dp"),
        P("dp"),
        P("dp", None),
        P("dp", None),
        P("dp", None),
        P("dp"),
        P("dp"),
        P("dp", None),
        P("dp"),
        P("dp"),
        P("dp"),
        P("dp", None),
        P("dp"),
        P("dp", None),
        P("dp"),
        P("dp"),
        P("dp"),
        P(("dp", "mod"), None, None),
        P(("dp", "mod"), None, None),
    )
    out_specs = (
        P(("dp", "mod"), None, None),
        P(("dp", "mod"), None, None),
        P(("dp", "mod"), None, None),
        P(("dp", "mod"), None, None),
        P("dp", None),
        P("dp"),
        P("dp"),
        P("dp", None),
        P("dp", None),
        P("dp", None),
        P("dp"),
        P("dp"),
        P("dp", None),
        P("dp"),
        P("dp"),
        P("dp"),
        P("dp", None),
        P("dp"),
        P("dp", None),
        P("dp"),
        P("dp"),
        P("dp"),
    )
    return jax.shard_map(body, mesh=mesh, in_specs=in_specs, out_specs=out_specs, check_vma=False)
```

```python
import functools

import jax
import jax.numpy as jnp
from jax import lax
from jax.experimental import pallas as pl
from jax.experimental.pallas import tpu as pltpu
from jax.sharding import PartitionSpec as P

HEADS = 12
FINE = 16
COARSE = 8
PAIR = 128
BOTH = ("dp", "mod")


def swapped(block, axis, distance):
    count = lax.axis_size(axis)
    route = []
    for low in range(count):
        high = low | 1 << distance
        if high != low and high < count:
            route += [(low, high), (high, low)]
    return lax.ppermute(block, axis, route)


def product(left_mat, right_mat):
    return jnp.dot(left_mat, right_mat, preferred_element_type=jnp.float32)


def inner_rows(left_mat, right_mat):
    return lax.dot_general(
        left_mat, right_mat, (((0,), (0,)), ((), ())), preferred_element_type=jnp.float32
    )


def outer_cols(left_mat, right_mat):
    return lax.dot_general(
        left_mat, right_mat, (((1,), (1,)), ((), ())), preferred_element_type=jnp.float32
    )


def norm_forward(hidden_in, gain_vec, bias_vec):
    average = jnp.mean(hidden_in, axis=-1, keepdims=True)
    centered = hidden_in - average
    variance = jnp.mean(centered * centered, axis=-1, keepdims=True)
    inverse = lax.rsqrt(variance + 1e-05)
    return centered * inverse * gain_vec + bias_vec, average, inverse


def norm_backward(grad_out, hidden_in, average, inverse, gain_vec):
    standard = (hidden_in - average) * inverse
    grad_gain = jnp.sum(grad_out * standard, 0)
    grad_bias = jnp.sum(grad_out, 0)
    scaled = grad_out * gain_vec
    mean_scaled = jnp.mean(scaled, axis=-1, keepdims=True)
    mean_cross = jnp.mean(scaled * standard, axis=-1, keepdims=True)
    grad_hidden = inverse * (scaled - mean_scaled - standard * mean_cross)
    return grad_hidden, grad_gain, grad_bias


def box_masks(boxes):
    left_edge = boxes[..., 0:1]
    top_edge = boxes[..., 1:2]
    right_edge = boxes[..., 2:3]
    bottom_edge = boxes[..., 3:4]
    fine_cell = jnp.arange(FINE * FINE, dtype=jnp.int32)
    fine_row = fine_cell // FINE
    fine_col = fine_cell % FINE
    inside_fine = (
        (fine_col >= left_edge)
        & (fine_col < right_edge)
        & (fine_row >= top_edge)
        & (fine_row < bottom_edge)
    )
    coarse_cell = jnp.arange(COARSE * COARSE, dtype=jnp.int32)
    coarse_row = coarse_cell // COARSE
    coarse_col = coarse_cell % COARSE
    inside_coarse = (
        (coarse_col >= left_edge // 2)
        & (coarse_col < (right_edge + 1) // 2)
        & (coarse_row >= top_edge // 2)
        & (coarse_row < (bottom_edge + 1) // 2)
    )
    coarse_area = jnp.sum(inside_coarse.astype(jnp.float32), -1, keepdims=True)
    fine_area = jnp.sum(inside_fine.astype(jnp.float32), -1, keepdims=True)
    return inside_coarse, inside_fine, coarse_area, fine_area


def key_live(counts_ref, page, text_slots, slots):
    col = lax.broadcasted_iota(jnp.int32, (1, slots), 1)
    text_count = counts_ref[page, 0]
    roi_count = counts_ref[page, 1]
    return (col < text_count) | ((col >= text_slots) & (col < text_slots + roi_count))


def attend_kernel(text_slots, scale, counts_ref, query_ref, key_ref, value_ref, out_ref, log_ref):
    slots = query_ref.shape[0]
    live = key_live(counts_ref, pl.program_id(0), text_slots, slots)
    lane = lax.broadcasted_iota(jnp.int32, (1, PAIR), 1)
    query = query_ref[...] * scale
    keys = key_ref[...]
    values = value_ref[...]
    parts = []
    logs = []
    for head in range(2):
        mine = (lane // (PAIR // 2)) == head
        masked = jnp.where(mine, query, jnp.zeros_like(query))
        scores = jnp.where(live, outer_cols(masked, keys), -1e30)
        highest = jnp.max(scores, -1, keepdims=True)
        exponent = jnp.exp(scores - highest)
        total = jnp.sum(exponent, -1, keepdims=True)
        weights = (exponent * (1.0 / total)).astype(jnp.bfloat16)
        parts.append(product(weights, values))
        logs.append(highest + jnp.log(total))
    first = lane < PAIR // 2
    out_ref[...] = jnp.where(first, parts[0], parts[1]).astype(jnp.bfloat16)
    log_ref[...] = jnp.where(first, logs[0], logs[1])


def attend_back_kernel(
    text_slots,
    scale,
    counts_ref,
    query_ref,
    key_ref,
    value_ref,
    grad_ref,
    log_ref,
    grad_query_ref,
    grad_key_ref,
    grad_value_ref,
):
    slots = query_ref.shape[0]
    live = key_live(counts_ref, pl.program_id(0), text_slots, slots)
    lane = lax.broadcasted_iota(jnp.int32, (1, PAIR), 1)
    query = query_ref[...] * scale
    keys = key_ref[...]
    values = value_ref[...]
    grad = grad_ref[...]
    logs = log_ref[...]
    queries_out = []
    keys_out = []
    values_out = []
    for head in range(2):
        mine = (lane // (PAIR // 2)) == head
        masked = jnp.where(mine, query, jnp.zeros_like(query))
        grad_mine = jnp.where(mine, grad, jnp.zeros_like(grad))
        log_col = logs[:, head * (PAIR // 2) : head * (PAIR // 2) + 1]
        weights = jnp.exp(jnp.where(live, outer_cols(masked, keys), -1e30) - log_col)
        grad_weights = outer_cols(grad_mine, values)
        delta = jnp.sum(grad_weights * weights, -1, keepdims=True)
        grad_scores = (weights * (grad_weights - delta)).astype(jnp.bfloat16)
        values_out.append(inner_rows(weights.astype(jnp.bfloat16), grad))
        queries_out.append(product(grad_scores, keys))
        keys_out.append(inner_rows(grad_scores, query))
    first = lane < PAIR // 2
    grad_query_ref[...] = (jnp.where(first, queries_out[0], queries_out[1]) * scale).astype(
        jnp.bfloat16
    )
    grad_key_ref[...] = jnp.where(first, keys_out[0], keys_out[1]).astype(jnp.bfloat16)
    grad_value_ref[...] = jnp.where(first, values_out[0], values_out[1]).astype(jnp.bfloat16)


def attention_call(kernel, counts, operands, out_types, page_count, flops):
    rows, width = operands[0].shape
    slots = rows // page_count
    spec = pl.BlockSpec((slots, PAIR), lambda page, pair, counts_ref: (page, pair))
    return pl.pallas_call(
        kernel,
        out_shape=tuple(jax.ShapeDtypeStruct((rows, width), kind) for kind in out_types),
        grid_spec=pltpu.PrefetchScalarGridSpec(
            num_scalar_prefetch=1,
            grid=(page_count, width // PAIR),
            in_specs=[spec] * len(operands),
            out_specs=tuple([spec] * len(out_types)),
        ),
        cost_estimate=pl.CostEstimate(
            flops=flops,
            bytes_accessed=rows * width * 2 * (len(operands) + len(out_types)),
            transcendentals=rows * slots * HEADS,
        ),
        compiler_params=pltpu.CompilerParams(
            dimension_semantics=("arbitrary", "arbitrary"), vmem_limit_bytes=40 << 20
        ),
    )(counts, *operands)


def gather_all(shard):
    mod_size = lax.axis_size("mod")
    piece = shard.shape[0] // mod_size
    mine = lax.dynamic_slice_in_dim(shard, lax.axis_index("mod") * piece, piece, 0)
    full = lax.all_gather(mine, BOTH, axis=0, tiled=True)
    return full.reshape(-1, *shard.shape)


def scatter_sum(stacked):
    dp_size, rows, width = stacked.shape
    return lax.psum_scatter(
        stacked.reshape(dp_size * rows, width), BOTH, scatter_dimension=0, tiled=True
    )


MESH = pl.DeviceIdType.MESH


def grid_sizes():
    dp_size = lax.axis_size("dp")
    mod_size = lax.axis_size("mod")
    short = 1 << ((dp_size.bit_length() - 1) // 2)
    return dp_size // short, short, mod_size // 2


def place(sizes):
    _, short, _ = sizes
    dp_index = lax.axis_index("dp")
    mod_index = lax.axis_index("mod")
    return dp_index // short, dp_index % short, mod_index // 2, mod_index % 2


def device_at(sizes, row, col, wide, core):
    return {"dp": row * sizes[1] + col, "mod": wide * 2 + core}


def greet(peers):
    barrier = pltpu.get_barrier_semaphore()
    for peer in peers:
        pl.semaphore_signal(barrier, inc=1, device_id=peer, device_id_type=MESH)
    pl.semaphore_wait(barrier, len(peers))


def send(source, target, send_sem, recv_sem, peer):
    copy = pltpu.make_async_remote_copy(
        src_ref=source,
        dst_ref=target,
        send_sem=send_sem,
        recv_sem=recv_sem,
        device_id=peer,
        device_id_type=MESH,
    )
    copy.start()
    return copy


def total_kernel(mod_size, dp_size, stats_ref, out_ref, near, far, send_sem, recv_sem):
    my_mod = lax.axis_index("mod")
    my_dp = lax.axis_index("dp")
    near_peers = [{"mod": (my_mod + step) % mod_size} for step in range(1, mod_size)]
    far_peers = [{"dp": (my_dp + step) % dp_size} for step in range(1, dp_size)]
    greet(near_peers + far_peers)
    near[my_mod] = stats_ref[...]
    copies = [
        send(stats_ref, near.at[my_mod], send_sem.at[at], recv_sem.at[at], peer)
        for at, peer in enumerate(near_peers)
    ]
    for copy in copies:
        copy.wait()
    group = near[0]
    for at in range(1, mod_size):
        group = group + near[at]
    far[my_dp] = group
    copies = [
        send(
            far.at[my_dp],
            far.at[my_dp],
            send_sem.at[mod_size - 1 + at],
            recv_sem.at[mod_size - 1 + at],
            peer,
        )
        for at, peer in enumerate(far_peers)
    ]
    for copy in copies:
        copy.wait()
    total = far[0]
    for at in range(1, dp_size):
        total = total + far[at]
    out_ref[...] = total


def total_sum(stats, call_id):
    mod_size = lax.axis_size("mod")
    dp_size = lax.axis_size("dp")
    messages = mod_size + dp_size - 2
    padded = jnp.pad(stats, ((0, -stats.shape[0] % 8), (0, 0)))
    vmem = pl.BlockSpec(memory_space=pltpu.VMEM)
    return pl.pallas_call(
        functools.partial(total_kernel, mod_size, dp_size),
        out_shape=jax.ShapeDtypeStruct(padded.shape, jnp.float32),
        in_specs=[vmem],
        out_specs=vmem,
        scratch_shapes=[
            pltpu.VMEM((mod_size, *padded.shape), jnp.float32),
            pltpu.VMEM((dp_size, *padded.shape), jnp.float32),
            pltpu.SemaphoreType.DMA((messages,)),
            pltpu.SemaphoreType.DMA((messages,)),
        ],
        compiler_params=pltpu.CompilerParams(
            collective_id=call_id, has_side_effects=True, vmem_limit_bytes=8 << 20
        ),
        name=f"total_{call_id}",
    )(padded)


def gather_kernel(sizes, shard_ref, out_ref, send_sem, recv_sem, local_sem):
    rows, cols, wides = sizes
    row, col, wide, core = place(sizes)
    row_peers = [((row + step) % rows, col, wide, core) for step in range(1, rows)]
    col_peers = [(row, (col + step) % cols, wide, core) for step in range(1, cols)]
    wide_peers = [(row, col, (wide + step) % wides, core) for step in range(1, wides)]
    partner = (row, col, wide, 1 - core)
    own = pltpu.make_async_copy(shard_ref, out_ref.at[row, col], local_sem)
    own.start()
    own.wait()
    greet(
        [device_at(sizes, *peer) for peer in row_peers + col_peers + wide_peers + [partner]]
    )
    used = [0]
    pending = []

    def push(source, target, peer):
        at = used[0]
        used[0] += 1
        return send(
            source, target, send_sem.at[at], recv_sem.at[at], device_at(sizes, *peer)
        )

    def arrive(copies):
        for copy in copies:
            copy.wait_recv()
        pending.extend(copies)

    split_rows = [
        push(shard_ref.at[core, 0, wide], out_ref.at[row, col, core, 0, wide], peer)
        for peer in row_peers
    ]
    whole_rows = [
        push(shard_ref.at[core, 1], out_ref.at[row, col, core, 1], peer) for peer in row_peers
    ]
    arrive(split_rows)
    view = out_ref.at[:, col, core, 0, wide]
    split_cols = [push(view, view, peer) for peer in col_peers]
    arrive(whole_rows)
    view = out_ref.at[:, col, core, 1]
    whole_cols = [push(view, view, peer) for peer in col_peers]
    arrive(split_cols)
    view = out_ref.at[:, :, core, 0, wide]
    split_wide = [push(view, view, peer) for peer in wide_peers]
    arrive(whole_cols)
    view = out_ref.at[:, :, core, 1]
    whole_core = [push(view, view, partner)]
    arrive(split_wide)
    view = out_ref.at[:, :, core, 0]
    split_core = [push(view, view, partner)]
    arrive(whole_core)
    arrive(split_core)
    for copy in pending:
        copy.wait_send()


def quick_gather(shard, call_id):
    sizes = grid_sizes()
    rows, cols, wides = sizes
    height, width = shard.shape
    part = height // (4 * wides)
    messages = 2 * (rows - 1) + 2 * (cols - 1) + (wides - 1) + 2
    vmem = pl.BlockSpec(memory_space=pltpu.VMEM)
    out = pl.pallas_call(
        functools.partial(gather_kernel, sizes),
        out_shape=jax.ShapeDtypeStruct((rows, cols, 2, 2, wides, part, width), shard.dtype),
        in_specs=[vmem],
        out_specs=vmem,
        scratch_shapes=[
            pltpu.SemaphoreType.DMA((messages,)),
            pltpu.SemaphoreType.DMA((messages,)),
            pltpu.SemaphoreType.DMA(()),
        ],
        compiler_params=pltpu.CompilerParams(
            collective_id=call_id, has_side_effects=True, vmem_limit_bytes=32 << 20
        ),
        name="gather_weights",
    )(shard.reshape(2, 2, wides, part, width))
    return out.reshape(rows * cols, height, width)


def add_into(target, base, extras):
    total = base.astype(jnp.float32)
    for extra in extras:
        total = total + extra.astype(jnp.float32)
    target[...] = total.astype(target.dtype)


def scatter_kernel(
    sizes,
    grad_ref,
    out_ref,
    core_in,
    core_sum,
    col_in,
    col_sum,
    row_in,
    row_sum,
    wide_in,
    other_wide_in,
    other_wide_sum,
    other_col_in,
    other_col_sum,
    other_row_in,
    send_sem,
    recv_sem,
):
    rows, cols, wides = sizes
    row, col, wide, core = place(sizes)
    row_peers = [((row + step) % rows, col, wide, core) for step in range(1, rows)]
    col_peers = [(row, (col + step) % cols, wide, core) for step in range(1, cols)]
    wide_peers = [(row, col, (wide + step) % wides, core) for step in range(1, wides)]
    cross_peers = [(row, col, (wide + step) % wides, 1 - core) for step in range(wides)]
    partner = cross_peers[0]
    greet(
        [device_at(sizes, *peer) for peer in row_peers + col_peers + wide_peers + cross_peers]
    )
    used = [0]
    pending = []

    def push(source, target, peer):
        at = used[0]
        used[0] += 1
        return send(
            source, target, send_sem.at[at], recv_sem.at[at], device_at(sizes, *peer)
        )

    def arrive(copies):
        for copy in copies:
            copy.wait_recv()
        pending.extend(copies)

    core_copies = [
        push(grad_ref.at[:, :, 1 - core, half], core_in.at[half], partner) for half in range(2)
    ]

    def fold_core(half):
        arrive([core_copies[half]])

        def step(at, carry):
            z = at // cols
            y = at % cols
            add_into(
                core_sum.at[half, z, y],
                grad_ref[z, y, core, half],
                [core_in[half, z, y]],
            )
            return carry

        lax.fori_loop(0, rows * cols, step, 0)

    fold_core(0)
    col_copies = [
        push(core_sum.at[0, :, peer[1]], col_in.at[at], peer) for at, peer in enumerate(col_peers)
    ]
    fold_core(1)
    other_wide_copies = [
        push(core_sum.at[1, :, :, peer[2]], other_wide_in.at[at], peer)
        for at, peer in enumerate(wide_peers)
    ]
    arrive(col_copies)

    def fold_col(z, carry):
        add_into(
            col_sum.at[z], core_sum[0, z, col], [col_in[at, z] for at in range(cols - 1)]
        )
        return carry

    lax.fori_loop(0, rows, fold_col, 0)
    row_copies = [
        push(col_sum.at[peer[0]], row_in.at[at], peer) for at, peer in enumerate(row_peers)
    ]
    arrive(other_wide_copies)

    def fold_other_wide(at, carry):
        z = at // cols
        y = at % cols
        add_into(
            other_wide_sum.at[z, y],
            core_sum[1, z, y, wide],
            [other_wide_in[peer, z, y] for peer in range(wides - 1)],
        )
        return carry

    lax.fori_loop(0, rows * cols, fold_other_wide, 0)
    other_col_copies = [
        push(other_wide_sum.at[:, peer[1]], other_col_in.at[at], peer)
        for at, peer in enumerate(col_peers)
    ]
    arrive(other_col_copies)

    def fold_other_col(z, carry):
        add_into(
            other_col_sum.at[z],
            other_wide_sum[z, col],
            [other_col_in[at, z] for at in range(cols - 1)],
        )
        return carry

    lax.fori_loop(0, rows, fold_other_col, 0)
    other_row_copies = [
        push(other_col_sum.at[peer[0]], other_row_in.at[at], peer)
        for at, peer in enumerate(row_peers)
    ]
    arrive(row_copies)
    add_into(row_sum, col_sum[row], [row_in[at] for at in range(rows - 1)])
    wide_copies = [
        push(row_sum.at[peer[2]], wide_in.at[at], peer) for at, peer in enumerate(wide_peers)
    ]
    arrive(other_row_copies)
    add_into(
        out_ref.at[core, 1, wide],
        other_col_sum[row],
        [other_row_in[at] for at in range(rows - 1)],
    )
    last = [
        push(out_ref.at[core, 1, wide], out_ref.at[core, 1, wide], peer)
        for peer in wide_peers + cross_peers
    ]
    arrive(wide_copies)
    add_into(
        out_ref.at[core, 0, wide], row_sum[wide], [wide_in[at] for at in range(wides - 1)]
    )
    last += [
        push(out_ref.at[core, 0, wide], out_ref.at[core, 0, wide], peer)
        for peer in wide_peers + cross_peers
    ]
    arrive(last)
    for copy in pending:
        copy.wait_send()


def quick_scatter(stacked, call_id):
    sizes = grid_sizes()
    rows, cols, wides = sizes
    _, height, width = stacked.shape
    part = height // (4 * wides)
    messages = (
        2 + 2 * (cols - 1) + 2 * (wides - 1) + 2 * (rows - 1) + 2 * (2 * wides - 1)
    )
    vmem = pl.BlockSpec(memory_space=pltpu.VMEM)
    kind = stacked.dtype

    def buffer(*shape):
        return pltpu.VMEM((*shape, part, width), kind)

    out = pl.pallas_call(
        functools.partial(scatter_kernel, sizes),
        out_shape=jax.ShapeDtypeStruct((2, 2, wides, part, width), kind),
        in_specs=[vmem],
        out_specs=vmem,
        scratch_shapes=[
            buffer(2, rows, cols, wides),
            buffer(2, rows, cols, wides),
            buffer(cols - 1, rows, wides),
            buffer(rows, wides),
            buffer(rows - 1, wides),
            buffer(wides),
            buffer(wides - 1),
            buffer(wides - 1, rows, cols),
            buffer(rows, cols),
            buffer(cols - 1, rows),
            buffer(rows),
            buffer(rows - 1),
            pltpu.SemaphoreType.DMA((messages,)),
            pltpu.SemaphoreType.DMA((messages,)),
        ],
        compiler_params=pltpu.CompilerParams(
            collective_id=call_id, has_side_effects=True, vmem_limit_bytes=56 << 20
        ),
        name="scatter_grads",
        cost_estimate=pl.CostEstimate(
            flops=stacked.size, bytes_accessed=32 * stacked.size, transcendentals=0
        ),
    )(stacked.reshape(rows, cols, 2, 2, wides, part, width))
    return out.reshape(height, width)


def body(
    text_emb,
    feature_maps,
    boxes,
    row_counts,
    w_roi,
    bn_gain,
    bn_bias,
    w_query,
    w_key,
    w_value,
    b_query,
    b_value,
    w_out,
    b_out,
    ln1_gain,
    ln1_bias,
    w_up,
    b_up,
    w_down,
    b_down,
    ln2_gain,
    ln2_bias,
    out_grad_text,
    out_grad_roi,
):
    page_count, text_slots, width = text_emb.shape
    roi_slots = boxes.shape[1]
    slots = text_slots + roi_slots
    channels = feature_maps.shape[2]
    head_size = width // HEADS
    scale = head_size ** (-0.5)
    coarse_cells = COARSE * COARSE
    rows = page_count * slots
    dp_size = lax.axis_size("dp")
    mod_size = lax.axis_size("mod")
    top_bit = mod_size.bit_length() - 2
    my_mod = lax.axis_index("mod")
    bf16 = jnp.bfloat16
    f32 = jnp.float32

    vectors = (
        bn_gain,
        bn_bias,
        b_query,
        b_value,
        b_out,
        ln1_gain,
        ln1_bias,
        b_down,
        ln2_gain,
        ln2_bias,
        b_up,
    )
    vector_len = sum(vector.shape[0] for vector in vectors)
    pieces = (w_roi, w_query, w_key, w_value)
    matrix_rows = sum(piece.shape[0] for piece in pieces)
    quantum = 32 * mod_size
    vector_rows = -(-(matrix_rows + -(-vector_len // width)) // quantum) * quantum - matrix_rows
    packed_vectors = jnp.pad(
        jnp.concatenate(vectors), (0, vector_rows * width - vector_len)
    ).reshape(vector_rows, width)
    first_full = quick_gather(jnp.concatenate([*pieces, packed_vectors], 0), 1)
    ff_parts = w_up.shape[1] // width
    up_blocks = w_up.reshape(w_up.shape[0], ff_parts, width).transpose(1, 0, 2)
    second_full = gather_all(
        jnp.concatenate([up_blocks.reshape(-1, width), w_down, w_out], 0)
    )

    far_maps, far_boxes, far_grad = swapped(
        (feature_maps, boxes, out_grad_roi), "mod", top_bit
    )
    counts = lax.dynamic_slice_in_dim(row_counts, my_mod * page_count, page_count, 0)
    text_live = jnp.arange(text_slots, dtype=jnp.int32)[None, :] < counts[:, 0:1]
    roi_live = jnp.arange(roi_slots, dtype=jnp.int32)[None, :] < counts[:, 1:2]
    live = jnp.concatenate([text_live, roi_live], 1).reshape(rows, 1).astype(f32)
    roi_mask = roi_live.reshape(-1, 1).astype(f32)

    def pooled_part(mask, maps, area):
        return (
            jnp.einsum("prc,pcf->prf", mask.astype(bf16), maps, preferred_element_type=f32) / area
        )

    coarse_in, fine_in, coarse_area, fine_area = box_masks(far_boxes)
    pooled = (
        jnp.concatenate(
            [
                pooled_part(coarse_in, far_maps[:, :coarse_cells], coarse_area),
                pooled_part(fine_in, far_maps[:, coarse_cells:], fine_area),
            ],
            -1,
        )
        .astype(bf16)
        .reshape(page_count * roi_slots, 2 * channels)
    )

    starts = []
    at = 0
    for piece in pieces:
        starts.append(at)
        at += piece.shape[0]

    def unpack(full, start, count):
        return full[:, start : start + count].reshape(dp_size * count, width)

    roi_weight, query_weight, key_weight, value_weight = (
        unpack(first_full, start, piece.shape[0]) for start, piece in zip(starts, pieces)
    )
    flat_vectors = first_full[:, matrix_rows:].reshape(dp_size, vector_rows * width)
    full_vectors = []
    at = 0
    for vector in vectors:
        full_vectors.append(
            flat_vectors[:, at : at + vector.shape[0]].reshape(-1).astype(f32)
        )
        at += vector.shape[0]
    (
        norm_gain,
        norm_bias,
        query_bias,
        value_bias,
        out_bias,
        first_gain,
        first_bias,
        down_bias,
        second_gain,
        second_bias,
        up_bias,
    ) = full_vectors
    up_rows = w_up.shape[0] * ff_parts
    up_weights = [
        unpack(second_full, part * w_up.shape[0], w_up.shape[0]) for part in range(ff_parts)
    ]
    down_weight = unpack(second_full, up_rows, w_down.shape[0])
    down_weights = [down_weight[part * width : (part + 1) * width] for part in range(ff_parts)]
    out_weight = unpack(second_full, up_rows + w_down.shape[0], w_out.shape[0])

    projected = product(pooled, roi_weight)
    stats = jnp.stack(
        [
            jnp.sum(projected * roi_mask, 0),
            jnp.sum(projected * projected * roi_mask, 0),
            jnp.broadcast_to(jnp.sum(roi_mask), (width,)),
        ]
    )
    stats = total_sum(stats, 2)
    number = stats[2:3]
    average = stats[0:1] / number
    variance = stats[1:2] / number - average * average
    inv_std = lax.rsqrt(variance + 1e-05)
    standard = (projected - average) * inv_std
    roi_rows = (standard * norm_gain + norm_bias).astype(bf16)
    rows_in = jnp.concatenate(
        [text_emb, roi_rows.reshape(page_count, roi_slots, width)], 1
    ).reshape(rows, width)
    queries = (product(rows_in, query_weight) + query_bias).astype(bf16)
    keys = product(rows_in, key_weight).astype(bf16)
    values = (product(rows_in, value_weight) + value_bias).astype(bf16)
    attention_flops = 4 * rows * slots * width
    context, logs = attention_call(
        functools.partial(attend_kernel, text_slots, scale),
        counts,
        (queries, keys, values),
        (bf16, f32),
        page_count,
        attention_flops,
    )
    first_in = rows_in.astype(f32) + product(context, out_weight) + out_bias
    normed, first_average, first_inverse = norm_forward(first_in, first_gain, first_bias)
    normed_low = normed.astype(bf16)
    activated = []
    slopes = []
    second_in = normed + down_bias
    for part in range(ff_parts):
        hidden = (
            product(normed_low, up_weights[part]) + up_bias[part * width : (part + 1) * width]
        )
        cumulative = 0.5 * (1.0 + lax.erf(hidden * (0.5**0.5)))
        activated.append((hidden * cumulative).astype(bf16))
        density = jnp.exp(-0.5 * hidden * hidden) * 0.3989422804014327
        slopes.append((cumulative + hidden * density).astype(bf16))
    for part in range(ff_parts):
        second_in = second_in + product(activated[part], down_weights[part])
    normed_out, second_average, second_inverse = norm_forward(
        second_in, second_gain, second_bias
    )
    output = (normed_out * live).astype(bf16).reshape(page_count, slots, width)
    out_text = output[:, :text_slots]
    out_roi = swapped(output[:, text_slots:], "mod", top_bit)

    upstream = (
        jnp.concatenate([out_grad_text, far_grad], 1).reshape(rows, width).astype(f32) * live
    )
    grad_second, grad_ln2_gain, grad_ln2_bias = norm_backward(
        upstream, second_in, second_average, second_inverse, second_gain
    )
    grad_mixed = grad_second.astype(bf16)
    grad_w_down = []
    grad_hidden = []
    grad_b_up = []
    grad_w_up = []
    for part in range(ff_parts):
        grad_w_down.append(inner_rows(activated[part], grad_mixed).astype(bf16))
        grad_hidden.append(
            (
                outer_cols(grad_mixed, down_weights[part]) * slopes[part].astype(f32)
            ).astype(bf16)
        )
        grad_b_up.append(jnp.sum(grad_hidden[part].astype(f32), 0))
        grad_w_up.append(inner_rows(normed_low, grad_hidden[part]).astype(bf16))
    grad_b_down = jnp.sum(grad_mixed.astype(f32), 0)
    down_stack = jnp.concatenate(grad_w_down, 0).reshape(dp_size, -1, width)
    second_part = scatter_sum(
        jnp.concatenate(
            [grad.reshape(dp_size, -1, width) for grad in grad_w_up] + [down_stack], 1
        )
    )
    grad_normed = grad_second
    for part in range(ff_parts):
        grad_normed = grad_normed + outer_cols(grad_hidden[part], up_weights[part])
    grad_first, grad_ln1_gain, grad_ln1_bias = norm_backward(
        grad_normed,
        first_in,
        first_average,
        first_inverse,
        first_gain,
    )
    grad_attended = grad_first.astype(bf16)
    grad_w_out = inner_rows(context, grad_attended).astype(bf16)
    grad_b_out = jnp.sum(grad_attended.astype(f32), 0)
    grad_context = outer_cols(grad_attended, out_weight).astype(bf16)
    grad_queries, grad_keys, grad_values = attention_call(
        functools.partial(attend_back_kernel, text_slots, scale),
        counts,
        (queries, keys, values, grad_context, logs),
        (bf16, bf16, bf16),
        page_count,
        attention_flops * 5 // 2,
    )
    grad_rows = (
        grad_first
        + outer_cols(grad_queries, query_weight)
        + outer_cols(grad_keys, key_weight)
        + outer_cols(grad_values, value_weight)
    ).reshape(page_count, slots, width)
    grad_text = grad_rows[:, :text_slots]
    grad_roi = grad_rows[:, text_slots:].reshape(page_count * roi_slots, width)
    grad_w_query = inner_rows(rows_in, grad_queries).astype(bf16)
    grad_b_query = jnp.sum(grad_queries.astype(f32), 0)
    grad_w_key = inner_rows(rows_in, grad_keys).astype(bf16)
    grad_w_value = inner_rows(rows_in, grad_values).astype(bf16)
    grad_b_value = jnp.sum(grad_values.astype(f32), 0)
    grad_vectors = (
        jnp.sum(grad_roi * standard, 0),
        jnp.sum(grad_roi, 0),
        grad_b_query,
        grad_b_value,
        grad_b_out,
        grad_ln1_gain,
        grad_ln1_bias,
        grad_b_down,
        grad_ln2_gain,
        grad_ln2_bias,
    )
    sums = total_sum(
        jnp.concatenate(
            [vector[None] for vector in (*grad_vectors, *grad_b_up)], 0
        ),
        3,
    )
    sum_scaled = sums[0:1]
    sum_grad = sums[1:2]
    grad_projected = (
        inv_std
        * (
            grad_roi * norm_gain
            - roi_mask * norm_gain * (sum_grad + standard * sum_scaled) / number
        )
    ).astype(bf16)
    grad_w_roi = inner_rows(pooled, grad_projected).astype(bf16)
    grad_pooled = (
        outer_cols(grad_projected, roi_weight)
        .astype(bf16)
        .reshape(page_count, roi_slots, 2 * channels)
    )
    own_pooled = swapped(grad_pooled, "mod", top_bit)
    own_coarse, own_fine, own_coarse_area, own_fine_area = box_masks(boxes)

    def spread(mask, grad, area):
        return jnp.einsum(
            "prc,prf->pcf",
            mask.astype(bf16),
            (grad.astype(f32) / area).astype(bf16),
            preferred_element_type=f32,
        )

    grad_maps = jnp.concatenate(
        [
            spread(own_coarse, own_pooled[..., :channels], own_coarse_area),
            spread(own_fine, own_pooled[..., channels:], own_fine_area),
        ],
        1,
    )

    first_share = quick_scatter(
        jnp.concatenate(
            [
                grad.reshape(dp_size, -1, width)
                for grad in (grad_w_roi, grad_w_query, grad_w_key, grad_w_value, grad_w_out)
            ],
            1,
        ),
        4,
    )
    second_part, first_share = lax.optimization_barrier((second_part, first_share))
    second_share = lax.all_gather(second_part, "mod", axis=0, tiled=True)
    first_share = first_share.astype(f32)
    own_matrices = []
    at = 0
    for piece in (*pieces, w_out):
        own_matrices.append(first_share[at : at + piece.shape[0]])
        at += piece.shape[0]
    own_w_roi, own_w_query, own_w_key, own_w_value, own_w_out = own_matrices
    own_w_up = (
        second_share[:up_rows]
        .reshape(ff_parts, w_up.shape[0], width)
        .transpose(1, 0, 2)
        .reshape(w_up.shape)
        .astype(f32)
    )
    own_w_down = second_share[up_rows:].astype(f32)
    my_dp = lax.axis_index("dp")
    share_len = width // dp_size
    vector_share = lax.dynamic_slice_in_dim(
        sums[: len(grad_vectors)], my_dp * share_len, share_len, 1
    )
    up_share = lax.dynamic_slice_in_dim(
        sums[len(grad_vectors) : len(grad_vectors) + ff_parts].reshape(-1),
        my_dp * b_up.shape[0],
        b_up.shape[0],
        0,
    )
    return (
        out_text,
        out_roi,
        grad_text,
        grad_maps,
        own_w_roi,
        vector_share[0],
        vector_share[1],
        own_w_query,
        own_w_key,
        own_w_value,
        vector_share[2],
        vector_share[3],
        own_w_out,
        vector_share[4],
        vector_share[5],
        vector_share[6],
        own_w_up,
        up_share,
        own_w_down,
        vector_share[7],
        vector_share[8],
        vector_share[9],
    )


def solution(mesh):
    in_specs = (
        P(("dp", "mod"), None, None),
        P(("dp", "mod"), None, None),
        P(("dp", "mod"), None, None),
        P("dp", None),
        P("dp", None),
        P("dp"),
        P("dp"),
        P("dp", None),
        P("dp", None),
        P("dp", None),
        P("dp"),
        P("dp"),
        P("dp", None),
        P("dp"),
        P("dp"),
        P("dp"),
        P("dp", None),
        P("dp"),
        P("dp", None),
        P("dp"),
        P("dp"),
        P("dp"),
        P(("dp", "mod"), None, None),
        P(("dp", "mod"), None, None),
    )
    out_specs = (
        P(("dp", "mod"), None, None),
        P(("dp", "mod"), None, None),
        P(("dp", "mod"), None, None),
        P(("dp", "mod"), None, None),
        P("dp", None),
        P("dp"),
        P("dp"),
        P("dp", None),
        P("dp", None),
        P("dp", None),
        P("dp"),
        P("dp"),
        P("dp", None),
        P("dp"),
        P("dp"),
        P("dp"),
        P("dp", None),
        P("dp"),
        P("dp", None),
        P("dp"),
        P("dp"),
        P("dp"),
    )
    return jax.shard_map(body, mesh=mesh, in_specs=in_specs, out_specs=out_specs, check_vma=False)
```

```python
import functools

import jax
import jax.numpy as jnp
from jax import lax
from jax.experimental import pallas as pl
from jax.experimental.pallas import tpu as pltpu
from jax.sharding import PartitionSpec as P

HEADS = 12
FINE = 16
COARSE = 8
PAIR = 128
BOTH = ("dp", "mod")


def swapped(block, axis, distance):
    count = lax.axis_size(axis)
    route = []
    for low in range(count):
        high = low | 1 << distance
        if high != low and high < count:
            route += [(low, high), (high, low)]
    return lax.ppermute(block, axis, route)


def product(left_mat, right_mat):
    return jnp.dot(left_mat, right_mat, preferred_element_type=jnp.float32)


def inner_rows(left_mat, right_mat):
    return lax.dot_general(
        left_mat, right_mat, (((0,), (0,)), ((), ())), preferred_element_type=jnp.float32
    )


def outer_cols(left_mat, right_mat):
    return lax.dot_general(
        left_mat, right_mat, (((1,), (1,)), ((), ())), preferred_element_type=jnp.float32
    )


def norm_forward(hidden_in, gain_vec, bias_vec):
    average = jnp.mean(hidden_in, axis=-1, keepdims=True)
    centered = hidden_in - average
    variance = jnp.mean(centered * centered, axis=-1, keepdims=True)
    inverse = lax.rsqrt(variance + 1e-05)
    return centered * inverse * gain_vec + bias_vec, average, inverse


def norm_backward(grad_out, hidden_in, average, inverse, gain_vec):
    standard = (hidden_in - average) * inverse
    grad_gain = jnp.sum(grad_out * standard, 0)
    grad_bias = jnp.sum(grad_out, 0)
    scaled = grad_out * gain_vec
    mean_scaled = jnp.mean(scaled, axis=-1, keepdims=True)
    mean_cross = jnp.mean(scaled * standard, axis=-1, keepdims=True)
    grad_hidden = inverse * (scaled - mean_scaled - standard * mean_cross)
    return grad_hidden, grad_gain, grad_bias


def box_masks(boxes):
    left_edge = boxes[..., 0:1]
    top_edge = boxes[..., 1:2]
    right_edge = boxes[..., 2:3]
    bottom_edge = boxes[..., 3:4]
    fine_cell = jnp.arange(FINE * FINE, dtype=jnp.int32)
    fine_row = fine_cell // FINE
    fine_col = fine_cell % FINE
    inside_fine = (
        (fine_col >= left_edge)
        & (fine_col < right_edge)
        & (fine_row >= top_edge)
        & (fine_row < bottom_edge)
    )
    coarse_cell = jnp.arange(COARSE * COARSE, dtype=jnp.int32)
    coarse_row = coarse_cell // COARSE
    coarse_col = coarse_cell % COARSE
    inside_coarse = (
        (coarse_col >= left_edge // 2)
        & (coarse_col < (right_edge + 1) // 2)
        & (coarse_row >= top_edge // 2)
        & (coarse_row < (bottom_edge + 1) // 2)
    )
    coarse_area = jnp.sum(inside_coarse.astype(jnp.float32), -1, keepdims=True)
    fine_area = jnp.sum(inside_fine.astype(jnp.float32), -1, keepdims=True)
    return inside_coarse, inside_fine, coarse_area, fine_area


def key_live(counts_ref, page, text_slots, slots):
    col = lax.broadcasted_iota(jnp.int32, (1, slots), 1)
    text_count = counts_ref[page, 0]
    roi_count = counts_ref[page, 1]
    return (col < text_count) | ((col >= text_slots) & (col < text_slots + roi_count))


def attend_kernel(text_slots, scale, counts_ref, query_ref, key_ref, value_ref, out_ref, log_ref):
    slots = query_ref.shape[0]
    live = key_live(counts_ref, pl.program_id(0), text_slots, slots)
    lane = lax.broadcasted_iota(jnp.int32, (1, PAIR), 1)
    query = query_ref[...] * scale
    keys = key_ref[...]
    values = value_ref[...]
    parts = []
    logs = []
    for head in range(2):
        mine = (lane // (PAIR // 2)) == head
        masked = jnp.where(mine, query, jnp.zeros_like(query))
        scores = jnp.where(live, outer_cols(masked, keys), -1e30)
        highest = jnp.max(scores, -1, keepdims=True)
        exponent = jnp.exp(scores - highest)
        total = jnp.sum(exponent, -1, keepdims=True)
        weights = (exponent * (1.0 / total)).astype(jnp.bfloat16)
        parts.append(product(weights, values))
        logs.append(highest + jnp.log(total))
    first = lane < PAIR // 2
    out_ref[...] = jnp.where(first, parts[0], parts[1]).astype(jnp.bfloat16)
    log_ref[...] = jnp.where(first, logs[0], logs[1])


def attend_back_kernel(
    text_slots,
    scale,
    counts_ref,
    query_ref,
    key_ref,
    value_ref,
    grad_ref,
    log_ref,
    grad_query_ref,
    grad_key_ref,
    grad_value_ref,
):
    slots = query_ref.shape[0]
    live = key_live(counts_ref, pl.program_id(0), text_slots, slots)
    lane = lax.broadcasted_iota(jnp.int32, (1, PAIR), 1)
    query = query_ref[...] * scale
    keys = key_ref[...]
    values = value_ref[...]
    grad = grad_ref[...]
    logs = log_ref[...]
    queries_out = []
    keys_out = []
    values_out = []
    for head in range(2):
        mine = (lane // (PAIR // 2)) == head
        masked = jnp.where(mine, query, jnp.zeros_like(query))
        grad_mine = jnp.where(mine, grad, jnp.zeros_like(grad))
        log_col = logs[:, head * (PAIR // 2) : head * (PAIR // 2) + 1]
        weights = jnp.exp(jnp.where(live, outer_cols(masked, keys), -1e30) - log_col)
        grad_weights = outer_cols(grad_mine, values)
        delta = jnp.sum(grad_weights * weights, -1, keepdims=True)
        grad_scores = (weights * (grad_weights - delta)).astype(jnp.bfloat16)
        values_out.append(inner_rows(weights.astype(jnp.bfloat16), grad))
        queries_out.append(product(grad_scores, keys))
        keys_out.append(inner_rows(grad_scores, query))
    first = lane < PAIR // 2
    grad_query_ref[...] = (jnp.where(first, queries_out[0], queries_out[1]) * scale).astype(
        jnp.bfloat16
    )
    grad_key_ref[...] = jnp.where(first, keys_out[0], keys_out[1]).astype(jnp.bfloat16)
    grad_value_ref[...] = jnp.where(first, values_out[0], values_out[1]).astype(jnp.bfloat16)


def attention_call(kernel, counts, operands, out_types, page_count, flops):
    rows, width = operands[0].shape
    slots = rows // page_count
    spec = pl.BlockSpec((slots, PAIR), lambda page, pair, counts_ref: (page, pair))
    return pl.pallas_call(
        kernel,
        out_shape=tuple(jax.ShapeDtypeStruct((rows, width), kind) for kind in out_types),
        grid_spec=pltpu.PrefetchScalarGridSpec(
            num_scalar_prefetch=1,
            grid=(page_count, width // PAIR),
            in_specs=[spec] * len(operands),
            out_specs=tuple([spec] * len(out_types)),
        ),
        cost_estimate=pl.CostEstimate(
            flops=flops,
            bytes_accessed=rows * width * 2 * (len(operands) + len(out_types)),
            transcendentals=rows * slots * HEADS,
        ),
        compiler_params=pltpu.CompilerParams(
            dimension_semantics=("arbitrary", "arbitrary"), vmem_limit_bytes=40 << 20
        ),
    )(counts, *operands)


def gather_all(shard):
    mod_size = lax.axis_size("mod")
    piece = shard.shape[0] // mod_size
    mine = lax.dynamic_slice_in_dim(shard, lax.axis_index("mod") * piece, piece, 0)
    full = lax.all_gather(mine, BOTH, axis=0, tiled=True)
    return full.reshape(-1, *shard.shape)


def scatter_sum(stacked):
    dp_size, rows, width = stacked.shape
    return lax.psum_scatter(
        stacked.reshape(dp_size * rows, width), BOTH, scatter_dimension=0, tiled=True
    )


MESH = pl.DeviceIdType.MESH


def grid_sizes():
    dp_size = lax.axis_size("dp")
    mod_size = lax.axis_size("mod")
    short = 1 << ((dp_size.bit_length() - 1) // 2)
    return dp_size // short, short, mod_size // 2


def place(sizes):
    _, short, _ = sizes
    dp_index = lax.axis_index("dp")
    mod_index = lax.axis_index("mod")
    return dp_index // short, dp_index % short, mod_index // 2, mod_index % 2


def device_at(sizes, row, col, wide, core):
    return {"dp": row * sizes[1] + col, "mod": wide * 2 + core}


def greet(peers):
    barrier = pltpu.get_barrier_semaphore()
    for peer in peers:
        pl.semaphore_signal(barrier, inc=1, device_id=peer, device_id_type=MESH)
    pl.semaphore_wait(barrier, len(peers))


def send(source, target, send_sem, recv_sem, peer):
    copy = pltpu.make_async_remote_copy(
        src_ref=source,
        dst_ref=target,
        send_sem=send_sem,
        recv_sem=recv_sem,
        device_id=peer,
        device_id_type=MESH,
    )
    copy.start()
    return copy


def total_kernel(mod_size, dp_size, stats_ref, out_ref, near, far, send_sem, recv_sem):
    my_mod = lax.axis_index("mod")
    my_dp = lax.axis_index("dp")
    near_peers = [{"mod": (my_mod + step) % mod_size} for step in range(1, mod_size)]
    far_peers = [{"dp": (my_dp + step) % dp_size} for step in range(1, dp_size)]
    greet(near_peers + far_peers)
    near[my_mod] = stats_ref[...]
    copies = [
        send(stats_ref, near.at[my_mod], send_sem.at[at], recv_sem.at[at], peer)
        for at, peer in enumerate(near_peers)
    ]
    for copy in copies:
        copy.wait()
    group = near[0]
    for at in range(1, mod_size):
        group = group + near[at]
    far[my_dp] = group
    copies = [
        send(
            far.at[my_dp],
            far.at[my_dp],
            send_sem.at[mod_size - 1 + at],
            recv_sem.at[mod_size - 1 + at],
            peer,
        )
        for at, peer in enumerate(far_peers)
    ]
    for copy in copies:
        copy.wait()
    total = far[0]
    for at in range(1, dp_size):
        total = total + far[at]
    out_ref[...] = total


def total_sum(stats, call_id):
    mod_size = lax.axis_size("mod")
    dp_size = lax.axis_size("dp")
    messages = mod_size + dp_size - 2
    padded = jnp.pad(stats, ((0, -stats.shape[0] % 8), (0, 0)))
    vmem = pl.BlockSpec(memory_space=pltpu.VMEM)
    return pl.pallas_call(
        functools.partial(total_kernel, mod_size, dp_size),
        out_shape=jax.ShapeDtypeStruct(padded.shape, jnp.float32),
        in_specs=[vmem],
        out_specs=vmem,
        scratch_shapes=[
            pltpu.VMEM((mod_size, *padded.shape), jnp.float32),
            pltpu.VMEM((dp_size, *padded.shape), jnp.float32),
            pltpu.SemaphoreType.DMA((messages,)),
            pltpu.SemaphoreType.DMA((messages,)),
        ],
        compiler_params=pltpu.CompilerParams(
            collective_id=call_id, has_side_effects=True, vmem_limit_bytes=8 << 20
        ),
        name=f"total_{call_id}",
    )(padded)


def gather_kernel(sizes, shard_ref, out_ref, send_sem, recv_sem, local_sem):
    rows, cols, wides = sizes
    row, col, wide, core = place(sizes)
    row_peers = [((row + step) % rows, col, wide, core) for step in range(1, rows)]
    col_peers = [(row, (col + step) % cols, wide, core) for step in range(1, cols)]
    wide_peers = [(row, col, (wide + step) % wides, core) for step in range(1, wides)]
    partner = (row, col, wide, 1 - core)
    own = pltpu.make_async_copy(shard_ref, out_ref.at[row, col], local_sem)
    own.start()
    own.wait()
    greet(
        [device_at(sizes, *peer) for peer in row_peers + col_peers + wide_peers + [partner]]
    )
    used = [0]
    pending = []

    def push(source, target, peer):
        at = used[0]
        used[0] += 1
        return send(
            source, target, send_sem.at[at], recv_sem.at[at], device_at(sizes, *peer)
        )

    def arrive(copies):
        for copy in copies:
            copy.wait_recv()
        pending.extend(copies)

    split_rows = [
        push(shard_ref.at[core, 0, wide], out_ref.at[row, col, core, 0, wide], peer)
        for peer in row_peers
    ]
    whole_rows = [
        push(shard_ref.at[core, 1], out_ref.at[row, col, core, 1], peer) for peer in row_peers
    ]
    arrive(split_rows)
    view = out_ref.at[:, col, core, 0, wide]
    split_cols = [push(view, view, peer) for peer in col_peers]
    arrive(whole_rows)
    view = out_ref.at[:, col, core, 1]
    whole_cols = [push(view, view, peer) for peer in col_peers]
    arrive(split_cols)
    view = out_ref.at[:, :, core, 0, wide]
    split_wide = [push(view, view, peer) for peer in wide_peers]
    arrive(whole_cols)
    view = out_ref.at[:, :, core, 1]
    whole_core = [push(view, view, partner)]
    arrive(split_wide)
    view = out_ref.at[:, :, core, 0]
    split_core = [push(view, view, partner)]
    arrive(whole_core)
    arrive(split_core)
    for copy in pending:
        copy.wait_send()


def quick_gather(shard, call_id):
    sizes = grid_sizes()
    rows, cols, wides = sizes
    height, width = shard.shape
    part = height // (4 * wides)
    messages = 2 * (rows - 1) + 2 * (cols - 1) + (wides - 1) + 2
    vmem = pl.BlockSpec(memory_space=pltpu.VMEM)
    out = pl.pallas_call(
        functools.partial(gather_kernel, sizes),
        out_shape=jax.ShapeDtypeStruct((rows, cols, 2, 2, wides, part, width), shard.dtype),
        in_specs=[vmem],
        out_specs=vmem,
        scratch_shapes=[
            pltpu.SemaphoreType.DMA((messages,)),
            pltpu.SemaphoreType.DMA((messages,)),
            pltpu.SemaphoreType.DMA(()),
        ],
        compiler_params=pltpu.CompilerParams(
            collective_id=call_id, has_side_effects=True, vmem_limit_bytes=32 << 20
        ),
        name="gather_weights",
    )(shard.reshape(2, 2, wides, part, width))
    return out.reshape(rows * cols, height, width)


def add_into(target, base, extras):
    total = base.astype(jnp.float32)
    for extra in extras:
        total = total + extra.astype(jnp.float32)
    target[...] = total.astype(target.dtype)


def scatter_kernel(
    sizes,
    grad_ref,
    vector_ref,
    out_ref,
    total_ref,
    core_in,
    core_sum,
    col_in,
    col_sum,
    row_in,
    row_sum,
    wide_in,
    other_wide_in,
    other_wide_sum,
    other_col_in,
    other_col_sum,
    other_row_in,
    near,
    far,
    send_sem,
    recv_sem,
):
    rows, cols, wides = sizes
    row, col, wide, core = place(sizes)
    row_peers = [((row + step) % rows, col, wide, core) for step in range(1, rows)]
    col_peers = [(row, (col + step) % cols, wide, core) for step in range(1, cols)]
    wide_peers = [(row, col, (wide + step) % wides, core) for step in range(1, wides)]
    cross_peers = [(row, col, (wide + step) % wides, 1 - core) for step in range(wides)]
    partner = cross_peers[0]
    my_dp = row * cols + col
    my_mod = wide * 2 + core
    dp_size = rows * cols
    far_peers = []
    for step in range(1, dp_size):
        peer_dp = (my_dp + step) % dp_size
        far_peers.append((peer_dp // cols, peer_dp % cols, wide, core))
    near_peers = wide_peers + cross_peers
    greet([device_at(sizes, *peer) for peer in far_peers + near_peers])
    used = [0]
    pending = []

    def push(source, target, peer):
        at = used[0]
        used[0] += 1
        return send(
            source, target, send_sem.at[at], recv_sem.at[at], device_at(sizes, *peer)
        )

    def arrive(copies):
        for copy in copies:
            copy.wait_recv()
        pending.extend(copies)

    core_copies = [
        push(grad_ref.at[:, :, 1 - core, half], core_in.at[half], partner) for half in range(2)
    ]

    def fold_core(half):
        arrive([core_copies[half]])

        def step(at, carry):
            z = at // cols
            y = at % cols
            add_into(
                core_sum.at[half, z, y],
                grad_ref[z, y, core, half],
                [core_in[half, z, y]],
            )
            return carry

        lax.fori_loop(0, rows * cols, step, 0)

    fold_core(0)
    col_copies = [
        push(core_sum.at[0, :, peer[1]], col_in.at[at], peer) for at, peer in enumerate(col_peers)
    ]
    near[my_mod] = vector_ref[...]
    near_copies = [push(vector_ref, near.at[my_mod], peer) for peer in near_peers]
    fold_core(1)
    other_wide_copies = [
        push(core_sum.at[1, :, :, peer[2]], other_wide_in.at[at], peer)
        for at, peer in enumerate(wide_peers)
    ]
    arrive(near_copies)
    group = near[0]
    for at in range(1, 2 * wides):
        group = group + near[at]
    far[my_dp] = group
    far_copies = [push(far.at[my_dp], far.at[my_dp], peer) for peer in far_peers]
    arrive(col_copies)

    def fold_col(z, carry):
        add_into(
            col_sum.at[z], core_sum[0, z, col], [col_in[at, z] for at in range(cols - 1)]
        )
        return carry

    lax.fori_loop(0, rows, fold_col, 0)
    row_copies = [
        push(col_sum.at[peer[0]], row_in.at[at], peer) for at, peer in enumerate(row_peers)
    ]
    arrive(other_wide_copies)

    def fold_other_wide(at, carry):
        z = at // cols
        y = at % cols
        add_into(
            other_wide_sum.at[z, y],
            core_sum[1, z, y, wide],
            [other_wide_in[peer, z, y] for peer in range(wides - 1)],
        )
        return carry

    lax.fori_loop(0, rows * cols, fold_other_wide, 0)
    other_col_copies = [
        push(other_wide_sum.at[:, peer[1]], other_col_in.at[at], peer)
        for at, peer in enumerate(col_peers)
    ]
    arrive(other_col_copies)

    def fold_other_col(z, carry):
        add_into(
            other_col_sum.at[z],
            other_wide_sum[z, col],
            [other_col_in[at, z] for at in range(cols - 1)],
        )
        return carry

    lax.fori_loop(0, rows, fold_other_col, 0)
    other_row_copies = [
        push(other_col_sum.at[peer[0]], other_row_in.at[at], peer)
        for at, peer in enumerate(row_peers)
    ]
    arrive(row_copies)
    add_into(row_sum, col_sum[row], [row_in[at] for at in range(rows - 1)])
    wide_copies = [
        push(row_sum.at[peer[2]], wide_in.at[at], peer) for at, peer in enumerate(wide_peers)
    ]
    arrive(other_row_copies)
    add_into(
        out_ref.at[core, 1, wide],
        other_col_sum[row],
        [other_row_in[at] for at in range(rows - 1)],
    )
    last = [
        push(out_ref.at[core, 1, wide], out_ref.at[core, 1, wide], peer)
        for peer in wide_peers + cross_peers
    ]
    arrive(wide_copies)
    add_into(
        out_ref.at[core, 0, wide], row_sum[wide], [wide_in[at] for at in range(wides - 1)]
    )
    last += [
        push(out_ref.at[core, 0, wide], out_ref.at[core, 0, wide], peer)
        for peer in wide_peers + cross_peers
    ]
    arrive(far_copies)
    total = far[0]
    for at in range(1, dp_size):
        total = total + far[at]
    total_ref[...] = total
    arrive(last)
    for copy in pending:
        copy.wait_send()


def quick_scatter(stacked, vectors, call_id):
    sizes = grid_sizes()
    rows, cols, wides = sizes
    _, height, width = stacked.shape
    part = height // (4 * wides)
    messages = (
        2 + 2 * (cols - 1) + 2 * (wides - 1) + 2 * (rows - 1) + 3 * (2 * wides - 1)
    ) + rows * cols - 1
    vectors = jnp.pad(vectors, ((0, -vectors.shape[0] % 8), (0, 0)))
    vmem = pl.BlockSpec(memory_space=pltpu.VMEM)
    kind = stacked.dtype

    def buffer(*shape):
        return pltpu.VMEM((*shape, part, width), kind)

    out, total = pl.pallas_call(
        functools.partial(scatter_kernel, sizes),
        out_shape=(
            jax.ShapeDtypeStruct((2, 2, wides, part, width), kind),
            jax.ShapeDtypeStruct(vectors.shape, jnp.float32),
        ),
        in_specs=[vmem, vmem],
        out_specs=(vmem, vmem),
        scratch_shapes=[
            buffer(2, rows, cols, wides),
            buffer(2, rows, cols, wides),
            buffer(cols - 1, rows, wides),
            buffer(rows, wides),
            buffer(rows - 1, wides),
            buffer(wides),
            buffer(wides - 1),
            buffer(wides - 1, rows, cols),
            buffer(rows, cols),
            buffer(cols - 1, rows),
            buffer(rows),
            buffer(rows - 1),
            pltpu.VMEM((2 * wides, *vectors.shape), jnp.float32),
            pltpu.VMEM((rows * cols, *vectors.shape), jnp.float32),
            pltpu.SemaphoreType.DMA((messages,)),
            pltpu.SemaphoreType.DMA((messages,)),
        ],
        compiler_params=pltpu.CompilerParams(
            collective_id=call_id, has_side_effects=True, vmem_limit_bytes=56 << 20
        ),
        name="scatter_grads",
        cost_estimate=pl.CostEstimate(
            flops=stacked.size, bytes_accessed=32 * stacked.size, transcendentals=0
        ),
    )(stacked.reshape(rows, cols, 2, 2, wides, part, width), vectors)
    return out.reshape(height, width), total


def share_kernel(sizes, part_ref, out_ref, send_sem, recv_sem, local_sem):
    _, _, wides = sizes
    row, col, wide, core = place(sizes)
    partner = (row, col, wide, 1 - core)
    own = pltpu.make_async_copy(part_ref, out_ref.at[wide, core], local_sem)
    own.start()
    own.wait()
    wide_peers = [(row, col, (wide + step) % wides, core) for step in range(1, wides)]
    greet([device_at(sizes, *peer) for peer in wide_peers + [partner]])
    copies = []
    for peer in wide_peers + [partner]:
        at = len(copies)
        copies.append(
            send(
                part_ref,
                out_ref.at[wide, core],
                send_sem.at[at],
                recv_sem.at[at],
                device_at(sizes, *peer),
            )
        )
    for step in range(1, wides):
        copies[step - 1].wait_recv()
        landed = out_ref.at[(wide + wides - step) % wides, core]
        at = len(copies)
        copies.append(
            send(
                landed, landed, send_sem.at[at], recv_sem.at[at], device_at(sizes, *partner)
            )
        )
    for copy in copies[wides - 1 :]:
        copy.wait_recv()
    for copy in copies:
        copy.wait_send()


def quick_share(part, call_id):
    sizes = grid_sizes()
    wides = sizes[2]
    messages = 2 * wides - 1
    vmem = pl.BlockSpec(memory_space=pltpu.VMEM)
    out = pl.pallas_call(
        functools.partial(share_kernel, sizes),
        out_shape=jax.ShapeDtypeStruct((wides, 2, *part.shape), part.dtype),
        in_specs=[vmem],
        out_specs=vmem,
        scratch_shapes=[
            pltpu.SemaphoreType.DMA((messages,)),
            pltpu.SemaphoreType.DMA((messages,)),
            pltpu.SemaphoreType.DMA(()),
        ],
        compiler_params=pltpu.CompilerParams(
            collective_id=call_id, has_side_effects=True, vmem_limit_bytes=8 << 20
        ),
        name="share_grads",
    )(part)
    return out.reshape(-1, part.shape[1])


def body(
    text_emb,
    feature_maps,
    boxes,
    row_counts,
    w_roi,
    bn_gain,
    bn_bias,
    w_query,
    w_key,
    w_value,
    b_query,
    b_value,
    w_out,
    b_out,
    ln1_gain,
    ln1_bias,
    w_up,
    b_up,
    w_down,
    b_down,
    ln2_gain,
    ln2_bias,
    out_grad_text,
    out_grad_roi,
):
    page_count, text_slots, width = text_emb.shape
    roi_slots = boxes.shape[1]
    slots = text_slots + roi_slots
    channels = feature_maps.shape[2]
    head_size = width // HEADS
    scale = head_size ** (-0.5)
    coarse_cells = COARSE * COARSE
    rows = page_count * slots
    dp_size = lax.axis_size("dp")
    mod_size = lax.axis_size("mod")
    top_bit = mod_size.bit_length() - 2
    my_mod = lax.axis_index("mod")
    bf16 = jnp.bfloat16
    f32 = jnp.float32

    vectors = (
        bn_gain,
        bn_bias,
        b_query,
        b_value,
        b_out,
        ln1_gain,
        ln1_bias,
        b_down,
        ln2_gain,
        ln2_bias,
        b_up,
    )
    vector_len = sum(vector.shape[0] for vector in vectors)
    pieces = (w_roi, w_query, w_key, w_value)
    matrix_rows = sum(piece.shape[0] for piece in pieces)
    quantum = 32 * mod_size
    vector_rows = -(-(matrix_rows + -(-vector_len // width)) // quantum) * quantum - matrix_rows
    packed_vectors = jnp.pad(
        jnp.concatenate(vectors), (0, vector_rows * width - vector_len)
    ).reshape(vector_rows, width)
    first_full = quick_gather(jnp.concatenate([*pieces, packed_vectors], 0), 1)
    ff_parts = w_up.shape[1] // width
    up_blocks = w_up.reshape(w_up.shape[0], ff_parts, width).transpose(1, 0, 2)
    second_full = gather_all(
        jnp.concatenate([up_blocks.reshape(-1, width), w_down, w_out], 0)
    )

    far_maps, far_boxes, far_grad = swapped(
        (feature_maps, boxes, out_grad_roi), "mod", top_bit
    )
    counts = lax.dynamic_slice_in_dim(row_counts, my_mod * page_count, page_count, 0)
    text_live = jnp.arange(text_slots, dtype=jnp.int32)[None, :] < counts[:, 0:1]
    roi_live = jnp.arange(roi_slots, dtype=jnp.int32)[None, :] < counts[:, 1:2]
    live = jnp.concatenate([text_live, roi_live], 1).reshape(rows, 1).astype(f32)
    roi_mask = roi_live.reshape(-1, 1).astype(f32)

    def pooled_part(mask, maps, area):
        return (
            jnp.einsum("prc,pcf->prf", mask.astype(bf16), maps, preferred_element_type=f32) / area
        )

    coarse_in, fine_in, coarse_area, fine_area = box_masks(far_boxes)
    pooled = (
        jnp.concatenate(
            [
                pooled_part(coarse_in, far_maps[:, :coarse_cells], coarse_area),
                pooled_part(fine_in, far_maps[:, coarse_cells:], fine_area),
            ],
            -1,
        )
        .astype(bf16)
        .reshape(page_count * roi_slots, 2 * channels)
    )

    starts = []
    at = 0
    for piece in pieces:
        starts.append(at)
        at += piece.shape[0]

    def unpack(full, start, count):
        return full[:, start : start + count].reshape(dp_size * count, width)

    roi_weight, query_weight, key_weight, value_weight = (
        unpack(first_full, start, piece.shape[0]) for start, piece in zip(starts, pieces)
    )
    flat_vectors = first_full[:, matrix_rows:].reshape(dp_size, vector_rows * width)
    full_vectors = []
    at = 0
    for vector in vectors:
        full_vectors.append(
            flat_vectors[:, at : at + vector.shape[0]].reshape(-1).astype(f32)
        )
        at += vector.shape[0]
    (
        norm_gain,
        norm_bias,
        query_bias,
        value_bias,
        out_bias,
        first_gain,
        first_bias,
        down_bias,
        second_gain,
        second_bias,
        up_bias,
    ) = full_vectors
    up_rows = w_up.shape[0] * ff_parts
    up_weights = [
        unpack(second_full, part * w_up.shape[0], w_up.shape[0]) for part in range(ff_parts)
    ]
    down_weight = unpack(second_full, up_rows, w_down.shape[0])
    down_weights = [down_weight[part * width : (part + 1) * width] for part in range(ff_parts)]
    out_weight = unpack(second_full, up_rows + w_down.shape[0], w_out.shape[0])

    projected = product(pooled, roi_weight)
    stats = jnp.stack(
        [
            jnp.sum(projected * roi_mask, 0),
            jnp.sum(projected * projected * roi_mask, 0),
            jnp.broadcast_to(jnp.sum(roi_mask), (width,)),
        ]
    )
    stats = total_sum(stats, 2)
    number = stats[2:3]
    average = stats[0:1] / number
    variance = stats[1:2] / number - average * average
    inv_std = lax.rsqrt(variance + 1e-05)
    standard = (projected - average) * inv_std
    roi_rows = (standard * norm_gain + norm_bias).astype(bf16)
    rows_in = jnp.concatenate(
        [text_emb, roi_rows.reshape(page_count, roi_slots, width)], 1
    ).reshape(rows, width)
    queries = (product(rows_in, query_weight) + query_bias).astype(bf16)
    keys = product(rows_in, key_weight).astype(bf16)
    values = (product(rows_in, value_weight) + value_bias).astype(bf16)
    attention_flops = 4 * rows * slots * width
    context, logs = attention_call(
        functools.partial(attend_kernel, text_slots, scale),
        counts,
        (queries, keys, values),
        (bf16, f32),
        page_count,
        attention_flops,
    )
    first_in = rows_in.astype(f32) + product(context, out_weight) + out_bias
    normed, first_average, first_inverse = norm_forward(first_in, first_gain, first_bias)
    normed_low = normed.astype(bf16)
    activated = []
    slopes = []
    second_in = normed + down_bias
    for part in range(ff_parts):
        hidden = (
            product(normed_low, up_weights[part]) + up_bias[part * width : (part + 1) * width]
        )
        cumulative = 0.5 * (1.0 + lax.erf(hidden * (0.5**0.5)))
        activated.append((hidden * cumulative).astype(bf16))
        density = jnp.exp(-0.5 * hidden * hidden) * 0.3989422804014327
        slopes.append((cumulative + hidden * density).astype(bf16))
    for part in range(ff_parts):
        second_in = second_in + product(activated[part], down_weights[part])
    normed_out, second_average, second_inverse = norm_forward(
        second_in, second_gain, second_bias
    )
    output = (normed_out * live).astype(bf16).reshape(page_count, slots, width)
    out_text = output[:, :text_slots]
    out_roi = swapped(output[:, text_slots:], "mod", top_bit)

    upstream = (
        jnp.concatenate([out_grad_text, far_grad], 1).reshape(rows, width).astype(f32) * live
    )
    grad_second, grad_ln2_gain, grad_ln2_bias = norm_backward(
        upstream, second_in, second_average, second_inverse, second_gain
    )
    grad_mixed = grad_second.astype(bf16)
    grad_w_down = []
    grad_hidden = []
    grad_b_up = []
    grad_w_up = []
    for part in range(ff_parts):
        grad_w_down.append(inner_rows(activated[part], grad_mixed).astype(bf16))
        grad_hidden.append(
            (
                outer_cols(grad_mixed, down_weights[part]) * slopes[part].astype(f32)
            ).astype(bf16)
        )
        grad_b_up.append(jnp.sum(grad_hidden[part].astype(f32), 0))
        grad_w_up.append(inner_rows(normed_low, grad_hidden[part]).astype(bf16))
    grad_b_down = jnp.sum(grad_mixed.astype(f32), 0)
    down_stack = jnp.concatenate(grad_w_down, 0).reshape(dp_size, -1, width)
    second_part = scatter_sum(
        jnp.concatenate(
            [grad.reshape(dp_size, -1, width) for grad in grad_w_up] + [down_stack], 1
        )
    )
    grad_normed = grad_second
    for part in range(ff_parts):
        grad_normed = grad_normed + outer_cols(grad_hidden[part], up_weights[part])
    grad_first, grad_ln1_gain, grad_ln1_bias = norm_backward(
        grad_normed,
        first_in,
        first_average,
        first_inverse,
        first_gain,
    )
    grad_attended = grad_first.astype(bf16)
    grad_w_out = inner_rows(context, grad_attended).astype(bf16)
    grad_b_out = jnp.sum(grad_attended.astype(f32), 0)
    grad_context = outer_cols(grad_attended, out_weight).astype(bf16)
    grad_queries, grad_keys, grad_values = attention_call(
        functools.partial(attend_back_kernel, text_slots, scale),
        counts,
        (queries, keys, values, grad_context, logs),
        (bf16, bf16, bf16),
        page_count,
        attention_flops * 5 // 2,
    )
    grad_rows = (
        grad_first
        + outer_cols(grad_queries, query_weight)
        + outer_cols(grad_keys, key_weight)
        + outer_cols(grad_values, value_weight)
    ).reshape(page_count, slots, width)
    grad_text = grad_rows[:, :text_slots]
    grad_roi = grad_rows[:, text_slots:].reshape(page_count * roi_slots, width)
    grad_w_query = inner_rows(rows_in, grad_queries).astype(bf16)
    grad_b_query = jnp.sum(grad_queries.astype(f32), 0)
    grad_w_key = inner_rows(rows_in, grad_keys).astype(bf16)
    grad_w_value = inner_rows(rows_in, grad_values).astype(bf16)
    grad_b_value = jnp.sum(grad_values.astype(f32), 0)
    sums = total_sum(
        jnp.stack([jnp.sum(grad_roi * standard, 0), jnp.sum(grad_roi, 0)]),
        3,
    )
    sum_scaled = sums[0:1]
    sum_grad = sums[1:2]
    grad_projected = (
        inv_std
        * (
            grad_roi * norm_gain
            - roi_mask * norm_gain * (sum_grad + standard * sum_scaled) / number
        )
    ).astype(bf16)
    grad_w_roi = inner_rows(pooled, grad_projected).astype(bf16)
    grad_pooled = (
        outer_cols(grad_projected, roi_weight)
        .astype(bf16)
        .reshape(page_count, roi_slots, 2 * channels)
    )
    own_pooled = swapped(grad_pooled, "mod", top_bit)
    first_stack = jnp.concatenate(
        [
            grad.reshape(dp_size, -1, width)
            for grad in (grad_w_roi, grad_w_query, grad_w_key, grad_w_value, grad_w_out)
        ],
        1,
    )
    grad_vectors = (
        grad_b_query,
        grad_b_value,
        grad_b_out,
        grad_ln1_gain,
        grad_ln1_bias,
        grad_b_down,
        grad_ln2_gain,
        grad_ln2_bias,
    )
    first_stack, own_pooled, out_roi = lax.optimization_barrier((first_stack, own_pooled, out_roi))
    first_share, vector_sums = quick_scatter(
        first_stack,
        jnp.concatenate([vector[None] for vector in (*grad_vectors, *grad_b_up)], 0),
        4,
    )
    second_part, first_share = lax.optimization_barrier((second_part, first_share))
    second_share = quick_share(second_part, 5)
    first_share = first_share.astype(f32)
    own_coarse, own_fine, own_coarse_area, own_fine_area = box_masks(boxes)

    def spread(mask, grad, area):
        return jnp.einsum(
            "prc,prf->pcf",
            mask.astype(bf16),
            (grad.astype(f32) / area).astype(bf16),
            preferred_element_type=f32,
        )

    grad_maps = jnp.concatenate(
        [
            spread(own_coarse, own_pooled[..., :channels], own_coarse_area),
            spread(own_fine, own_pooled[..., channels:], own_fine_area),
        ],
        1,
    )

    own_matrices = []
    at = 0
    for piece in (*pieces, w_out):
        own_matrices.append(first_share[at : at + piece.shape[0]])
        at += piece.shape[0]
    own_w_roi, own_w_query, own_w_key, own_w_value, own_w_out = own_matrices
    own_w_up = (
        second_share[:up_rows]
        .reshape(ff_parts, w_up.shape[0], width)
        .transpose(1, 0, 2)
        .reshape(w_up.shape)
        .astype(f32)
    )
    own_w_down = second_share[up_rows:].astype(f32)
    my_dp = lax.axis_index("dp")
    share_len = width // dp_size
    norm_share = lax.dynamic_slice_in_dim(sums, my_dp * share_len, share_len, 1)
    vector_share = lax.dynamic_slice_in_dim(
        vector_sums[: len(grad_vectors)], my_dp * share_len, share_len, 1
    )
    up_share = lax.dynamic_slice_in_dim(
        vector_sums[len(grad_vectors) : len(grad_vectors) + ff_parts].reshape(-1),
        my_dp * b_up.shape[0],
        b_up.shape[0],
        0,
    )
    return (
        out_text,
        out_roi,
        grad_text,
        grad_maps,
        own_w_roi,
        norm_share[0],
        norm_share[1],
        own_w_query,
        own_w_key,
        own_w_value,
        vector_share[0],
        vector_share[1],
        own_w_out,
        vector_share[2],
        vector_share[3],
        vector_share[4],
        own_w_up,
        up_share,
        own_w_down,
        vector_share[5],
        vector_share[6],
        vector_share[7],
    )


def solution(mesh):
    in_specs = (
        P(("dp", "mod"), None, None),
        P(("dp", "mod"), None, None),
        P(("dp", "mod"), None, None),
        P("dp", None),
        P("dp", None),
        P("dp"),
        P("dp"),
        P("dp", None),
        P("dp", None),
        P("dp", None),
        P("dp"),
        P("dp"),
        P("dp", None),
        P("dp"),
        P("dp"),
        P("dp"),
        P("dp", None),
        P("dp"),
        P("dp", None),
        P("dp"),
        P("dp"),
        P("dp"),
        P(("dp", "mod"), None, None),
        P(("dp", "mod"), None, None),
    )
    out_specs = (
        P(("dp", "mod"), None, None),
        P(("dp", "mod"), None, None),
        P(("dp", "mod"), None, None),
        P(("dp", "mod"), None, None),
        P("dp", None),
        P("dp"),
        P("dp"),
        P("dp", None),
        P("dp", None),
        P("dp", None),
        P("dp"),
        P("dp"),
        P("dp", None),
        P("dp"),
        P("dp"),
        P("dp"),
        P("dp", None),
        P("dp"),
        P("dp", None),
        P("dp"),
        P("dp"),
        P("dp"),
    )
    return jax.shard_map(body, mesh=mesh, in_specs=in_specs, out_specs=out_specs, check_vma=False)
```
